32 devices in a mesh: pen: 16 (over z, x, core), gz: 2 (over y).
Axes of the slice: x: 2, y: 2, z: 4, core: 2. Of those that a mesh axis runs over, the one named last changes fastest.
Arguments:
- velocity: float32 [3, 2, 1024, 2048], P(None, 'gz', 'pen'), may hold values from -2.1 to 3.6
- inv_span: float32 [2], P('gz'), may hold values from 0.3 to 1.2
- sample_cell: int32 [2, 1024, 128], P('gz', 'pen'), may hold values from 0 to 131071
- sample_turbine: int32 [2, 1024, 1], P('gz', 'pen'), may hold values from 0 to 31; in each aligned block of 64 rows (0 to 63, 64 to 127, ..., all dimensions but the last counted through in order) at most 2 rows name the same one
- sample_weight: float32 [2, 1024, 128], P('gz', 'pen'), may hold values from 0.1 to 1
- thrust: float32 [32], replicated, may hold values from 0.75 to 2
Outputs:
- tendency: float32 [3, 2, 1024, 2048], P(None, 'gz', 'pen')
- velocity_next: float32 [3, 2, 1024, 2048], P(None, 'gz', 'pen')
The draws below stay inside these ranges and needn't reach their ends.
Inputs may be any that keep to these rules, and one draw needn't show every extreme that they name: `sample_turbine`: within the rows of one device (an aligned block of 64 rows) no turbine is named more than 2 times, a bound that some block reaches; every turbine is named by some row.
All inputs are finite; a program needn't handle non-finite values.
Results may differ from the reference program's by a relative error of at most 0.000094.
Values sent between devices are 32-bit elements; how exact they have to be, the bound alone decides.
No kernel may reach another device: no remote copies, remote signals or barrier semaphores. Data moves between devices by JAX's collectives and lax.ppermute only.
A program may use at most 192 MiB of HBM per device.

```python
import math
import jax
import jax.numpy as jnp
import numpy as np

NX = 2048
NY = 1024
CZ = 1
SROWS = 64
SAMP = 128
CAP = 2
CY = 64
NZ = 2
TURBINES = 32
N_PEN = 16
N_GZ = 2


def draw_velocity(key, part):
    first = jax.random.fold_in(key, 0)
    noise = 0.7 * jnp.clip(jax.random.normal(first, (3, NZ, NY, NX), jnp.float32), -3.0, 3.0)
    offset = jnp.array([1.5, 0.0, 0.0], jnp.float32)[:, None, None, None]
    return noise + offset


def with_ends(entries, key, least, high):
    longest = entries.shape.index(max(entries.shape))
    spots = []
    for shift in (0, 1):
        where = [jax.random.randint(jax.random.fold_in(key, axis), (), 0, length) for axis, length in enumerate(entries.shape)]
        where[longest] = (where[longest] + shift) % entries.shape[longest]
        spots.append(tuple(where))
    return entries.at[spots[0]].set(least).at[spots[1]].set(high)


def level_of(stream_key, dims, cuts, smallest, top_value):
    loudness = 1.0
    for position, blocks in cuts:
        heights = jax.random.uniform(jax.random.fold_in(jax.random.fold_in(stream_key, 6), position), (blocks,), jnp.float32, smallest / len(cuts), top_value / len(cuts))
        loudness = loudness * jnp.repeat(jnp.exp(heights), dims[position] // blocks).reshape((-1,) + (1,) * (len(dims) - 1 - position))
    return loudness


def shared_out(key, own, number, rows, number_of, top, reach, slope):
    order = jax.random.permutation(key, number_of)
    packed, usual = load_shares(number_of, rows * top, reach, slope, True), load_shares(number_of, rows * top, reach, slope, False)
    places = jnp.arange(number_of)

    def named(tallies, rotation):
        used = int((tallies > 0).sum())
        fixed = max(1, used // 4)
        moved = fixed + (places - fixed + rotation * (used - fixed)) % max(1, number_of - fixed)
        return jnp.zeros((number_of,), jnp.int32).at[order[jnp.where(places < fixed, places, moved)]].set(jnp.asarray(tallies, jnp.int32))

    tallies = jnp.where(number % 4 == 0, named(packed, number // 4), named(usual, number - number // 4 - 1))
    mixed = jax.random.permutation(jax.random.fold_in(own, 3), number_of)
    giver, receiver = mixed[0:number_of // 2 * 2:2], mixed[1:number_of // 2 * 2:2]
    margin = jnp.minimum(tallies[giver] - 1, reach - tallies[receiver]) // 2
    margin = jnp.where((giver == order[0]) | (receiver == order[0]) | (tallies[receiver] == 0), 0, jnp.maximum(margin, 0))
    moved = jax.random.randint(jax.random.fold_in(own, 4), (number_of // 2,), 0, 1 << 20) % (margin + 1)
    tallies = tallies.at[giver].add(-moved).at[receiver].add(moved)
    members = jnp.searchsorted(jnp.cumsum(tallies), jnp.arange(rows * top), side="right").astype(jnp.int32)
    grid = members.reshape(top, rows).T
    grid = grid[jax.random.permutation(jax.random.fold_in(own, 1), rows)]
    rotation = jax.random.randint(jax.random.fold_in(own, 2), (rows, 1), 0, top)
    return jnp.take_along_axis(grid, (jnp.arange(top)[None, :] + rotation) % top, axis=1)


def load_shares(number_of, total, limit, slope, full):
    loads = [(1 << 20) // math.isqrt(rank ** slope) + 1 for rank in range(1, number_of + 1)]
    largest = limit if full else min(limit, max(-(-total // number_of), total * loads[0] // sum(loads)))
    least = 1 if total - largest >= number_of - 1 else 0
    given, rest = [largest] + [least] * (number_of - 1), total - largest - least * (number_of - 1)
    while rest > 0:
        movable = [i for i in range(1, number_of) if given[i] < largest] or [i for i in range(1, number_of) if given[i] < limit]
        whole, left = sum([loads[i] for i in movable]), rest
        for i in movable:
            extra = min(limit - given[i], max(1, left * loads[i] // whole), rest)
            given[i] = given[i] + extra
            rest = rest - extra
    return np.array(given)


def setup_inputs(seed: int = 0) -> dict:
    keys = jax.random.split(jax.random.key(seed), 7)
    velocity = draw_velocity(jax.random.fold_in(keys[6], 71), 0)
    inv_span = jnp.clip(jnp.exp(math.log(1.2) - 1.3862944 * jax.random.uniform(keys[1], (NZ,), jnp.float32) ** level_of(keys[1], (NZ,), ((0, 2),), -0.2, 0.2)), 0.3, 1.2)
    sample_cell = with_ends(jax.random.randint(keys[2], (N_GZ, N_PEN * SROWS, SAMP), 0, CZ * CY * NX), jax.random.fold_in(keys[2], 1), 0, (CZ * CY * NX) - 1).astype(jnp.int32)
    sample_turbine_keys = jax.random.split(jax.random.fold_in(keys[3], 1), N_GZ * (N_PEN * SROWS) // SROWS)
    sample_turbine_turns = jax.random.permutation(jax.random.fold_in(keys[3], 3), N_GZ * (N_PEN * SROWS) // SROWS)
    sample_turbine = jax.vmap(lambda own, number: shared_out(jax.random.fold_in(keys[3], 2), own, number, SROWS, TURBINES, 1, CAP, 2))(sample_turbine_keys, sample_turbine_turns).reshape((N_GZ, N_PEN * SROWS, 1))
    sample_weight = jnp.clip(jnp.exp(math.log(1.0) - 2.3025851 * jax.random.uniform(keys[4], (N_GZ, N_PEN * SROWS, SAMP), jnp.float32) ** level_of(keys[4], (N_GZ, N_PEN * SROWS, SAMP), ((0, 2), (1, 16)), -0.2, 0.2)), 0.1, 1.0)
    thrust = jnp.clip(jax.random.uniform(keys[5], (TURBINES,), jnp.float32, 0.75, 2.0), 0.75, 2.0)
    return {"velocity": velocity, "inv_span": inv_span, "sample_cell": sample_cell, "sample_turbine": sample_turbine, "sample_weight": sample_weight, "thrust": thrust}


SECTION = 0.1


def inverse_field(spectrum, length_y, length_x):
    return jnp.fft.irfft2(spectrum, s=(length_y, length_x), axes=(-2, -1)).astype(jnp.float32)


def vertical(field, inv_span):
    padded = jnp.pad(field, ((1, 1), (0, 0), (0, 0)))
    return (padded[2:] - padded[:-2]) * inv_span[:, None, None]


def reference(velocity, inv_span, sample_cell, sample_turbine, sample_weight, thrust):
    length_z = velocity.shape[1]
    length_y = velocity.shape[2]
    length_x = velocity.shape[3]
    spectra = jnp.fft.rfft2(velocity, axes=(-2, -1))
    wave_index = jnp.arange(length_x // 2 + 1, dtype=jnp.int32)
    row_index = jnp.arange(length_y, dtype=jnp.int32)
    signed_rows = jnp.where(row_index <= length_y // 2, row_index, row_index - length_y)
    keeping = (3 * jnp.abs(signed_rows)[:, None] < length_y) & (3 * wave_index[None, :] < length_x)
    spectra = jnp.where(keeping, spectra, jnp.zeros_like(spectra))
    wave_x = (2.0 * math.pi / length_x) * wave_index.astype(jnp.float32)
    wave_y = ((2.0 * math.pi / length_y) * signed_rows.astype(jnp.float32))[:, None]
    smooth_u = inverse_field(spectra[0], length_y, length_x)
    smooth_v = inverse_field(spectra[1], length_y, length_x)
    smooth_w = inverse_field(spectra[2], length_y, length_x)
    spin_z = inverse_field(1j * wave_x * spectra[1] - 1j * wave_y * spectra[0], length_y, length_x)
    w_slope_x = inverse_field(1j * wave_x * spectra[2], length_y, length_x)
    w_slope_y = inverse_field(1j * wave_y * spectra[2], length_y, length_x)
    u_slope_z = vertical(velocity[0], inv_span)
    v_slope_z = vertical(velocity[1], inv_span)
    spin_x = w_slope_y - v_slope_z
    spin_y = u_slope_z - w_slope_x

    per_y = length_y // N_PEN
    per_z = length_z // N_GZ
    slab_index = jnp.arange(N_GZ, dtype=jnp.int32)[:, None, None]
    block_index = (jnp.arange(N_PEN * SROWS, dtype=jnp.int32) // SROWS)[None, :, None]
    grid_level = slab_index * per_z + sample_cell // (per_y * length_x)
    grid_row = block_index * per_y + (sample_cell // length_x) % per_y
    grid_column = sample_cell % length_x
    flat_index = ((grid_level * length_y + grid_row) * length_x + grid_column).astype(jnp.int32).reshape(-1)
    weights = sample_weight.reshape(-1, SAMP)
    picked = velocity[0].reshape(-1)[flat_index].reshape(-1, SAMP)
    row_numerator = jnp.sum(weights * picked, axis=1)
    row_denominator = jnp.sum(weights, axis=1)
    owners = sample_turbine.reshape(-1).astype(jnp.int32)
    numerator = jax.ops.segment_sum(row_numerator, owners, num_segments=TURBINES)
    denominator = jax.ops.segment_sum(row_denominator, owners, num_segments=TURBINES)
    disk_speed = numerator / denominator
    disk_force = -0.5 * thrust * disk_speed * jnp.abs(disk_speed)
    cell_force = (disk_force[owners][:, None] * weights).reshape(-1)
    push_x = jnp.zeros((length_z * length_y * length_x,), jnp.float32).at[flat_index].add(cell_force)
    push_x = push_x.reshape(length_z, length_y, length_x)

    tendency = jnp.stack([
        smooth_v * spin_z - smooth_w * spin_y + push_x,
        smooth_w * spin_x - smooth_u * spin_z,
        smooth_u * spin_y - smooth_v * spin_x,
    ])
    velocity_next = velocity + SECTION * tendency
    return tendency, velocity_next
```

```python
import functools
import math

import jax
import jax.numpy as jnp
import numpy as np
from jax import lax
from jax.experimental import pallas as pl
from jax.experimental.pallas import tpu as pltpu
from jax.sharding import PartitionSpec as P

SAMP = 128


SECTION = 0.1
EXACT = lax.Precision.HIGHEST
RADIX_X = 64
RADIX_Y = 32


def padded(value, sides, width):
    for axis, dim in sides:
        size, length = (lax.axis_size(axis), value.shape[dim])
        up = [(i, (i + 1) % size) for i in range(size - 1)]
        down = [(j, i) for i, j in up]
        last = lax.slice_in_dim(value, length - width, length, axis=dim)
        first = lax.slice_in_dim(value, 0, width, axis=dim)
        before = lax.ppermute(last, axis, up)
        after = lax.ppermute(first, axis, down)
        value = jnp.concatenate([before, value, after], axis=dim)
    return value


def pair_table(first_index, second_index, length):
    angles = (first_index * second_index % length).astype(jnp.float32) * (2.0 * math.pi / length)
    return (jnp.cos(angles), jnp.sin(angles))


def shards(velocity, inv_span, sample_cell, sample_turbine, sample_weight, thrust):
    components, levels, rows_here, length_x = velocity.shape
    pen_size = lax.axis_size("pen")
    length_y = rows_here * pen_size
    top_y = (length_y - 1) // 3
    width_y = (2 * top_y + 128) // 128 * 128
    count = -(-((length_x - 1) // 3 + 1) // pen_size) * pen_size
    local = count // pen_size
    inner_x = length_x // RADIX_X
    blocks_x = -(-count // RADIX_X)
    cos_one_x, sin_one_x = pair_table(
        jnp.arange(RADIX_X, dtype=jnp.int32)[:, None],
        jnp.arange(RADIX_X, dtype=jnp.int32)[None, :],
        RADIX_X,
    )
    wave_slots = (
        jnp.arange(RADIX_X, dtype=jnp.int32)[None, :, None]
        + RADIX_X * jnp.arange(blocks_x, dtype=jnp.int32)[None, None, :]
    )
    cos_two_x, sin_two_x = pair_table(
        jnp.arange(inner_x, dtype=jnp.int32)[:, None, None], wave_slots, length_x
    )
    inner_y = length_y // RADIX_Y
    blocks_y = -(-width_y // RADIX_Y)
    cos_one_y, sin_one_y = pair_table(
        jnp.arange(RADIX_Y, dtype=jnp.int32)[:, None],
        jnp.arange(RADIX_Y, dtype=jnp.int32)[None, :] - top_y,
        RADIX_Y,
    )
    slot_grid = (
        jnp.arange(RADIX_Y, dtype=jnp.int32)[None, :, None]
        + RADIX_Y * jnp.arange(blocks_y, dtype=jnp.int32)[None, None, :]
    )
    usable = (slot_grid <= 2 * top_y).astype(jnp.float32)
    cos_two_y, sin_two_y = pair_table(
        jnp.arange(inner_y, dtype=jnp.int32)[:, None, None], slot_grid - top_y, length_y
    )
    cos_two_y = cos_two_y * usable
    sin_two_y = sin_two_y * usable
    wave_y = (jnp.arange(width_y, dtype=jnp.int32) - top_y).astype(jnp.float32) * (
        2.0 * math.pi / length_y
    )
    first_mode = lax.axis_index("pen") * local
    kept_x = (3 * (first_mode + jnp.arange(local, dtype=jnp.int32)) < length_x).astype(jnp.float32)
    rims = padded(velocity[:2], (("gz", 1),), 1)
    slopes_z = (rims[:, 2:] - rims[:, :-2]) * inv_span[None, :, None, None]
    folded = velocity.reshape(components, levels, rows_here, RADIX_X, inner_x)
    section_re = jnp.einsum("czyji,jk->czyik", folded, cos_one_x, precision=EXACT)
    section_im = -jnp.einsum("czyji,jk->czyik", folded, sin_one_x, precision=EXACT)
    four_re = jnp.einsum("czyik,ikm->czymk", section_re, cos_two_x, precision=EXACT) + jnp.einsum(
        "czyik,ikm->czymk", section_im, sin_two_x, precision=EXACT
    )
    four_im = jnp.einsum("czyik,ikm->czymk", section_im, cos_two_x, precision=EXACT) - jnp.einsum(
        "czyik,ikm->czymk", section_re, sin_two_x, precision=EXACT
    )
    spectra = jnp.stack([four_re, four_im], axis=1).reshape(
        components, 2, levels, rows_here, blocks_x * RADIX_X
    )
    spectra = jnp.transpose(spectra[..., :count], (0, 1, 2, 4, 3))
    spectra = spectra.reshape(components, 2, levels, 1, count * rows_here)
    pencil_block = lax.all_to_all(spectra, "pen", split_axis=4, concat_axis=3, tiled=True)
    depth_here = pencil_block.shape[2]
    pencils = pencil_block.reshape(components, 2, depth_here, pen_size, local, rows_here)
    lines = jnp.transpose(pencils, (0, 1, 2, 4, 3, 5)).reshape(
        components, 2, depth_here, local, RADIX_Y, inner_y
    )
    line_re = lines[:, 0]
    line_im = lines[:, 1]
    part_re = jnp.einsum("czkji,js->czkis", line_re, cos_one_y, precision=EXACT) + jnp.einsum(
        "czkji,js->czkis", line_im, sin_one_y, precision=EXACT
    )
    part_im = jnp.einsum("czkji,js->czkis", line_im, cos_one_y, precision=EXACT) - jnp.einsum(
        "czkji,js->czkis", line_re, sin_one_y, precision=EXACT
    )
    mode_re = jnp.einsum("czkis,ist->czkts", part_re, cos_two_y, precision=EXACT) + jnp.einsum(
        "czkis,ist->czkts", part_im, sin_two_y, precision=EXACT
    )
    mode_im = jnp.einsum("czkis,ist->czkts", part_im, cos_two_y, precision=EXACT) - jnp.einsum(
        "czkis,ist->czkts", part_re, sin_two_y, precision=EXACT
    )
    mode_values = jnp.stack([mode_re, mode_im], axis=1).reshape(
        components, 2, depth_here, local, blocks_y * RADIX_Y
    )
    mode_values = mode_values * kept_x[None, None, None, :, None]
    paired = jnp.stack([mode_values[0], mode_values[2]])
    slopes = jnp.stack([-wave_y * paired[:, 1], wave_y * paired[:, 0]], axis=1)
    stacked = jnp.concatenate([mode_values, slopes], axis=0) * (1.0 / length_y)
    stacked = stacked.reshape(5, 2, depth_here, local, blocks_y, RADIX_Y)
    back_re = stacked[:, 0]
    back_im = stacked[:, 1]
    half_re = jnp.einsum("fzkts,ist->fzkis", back_re, cos_two_y, precision=EXACT) - jnp.einsum(
        "fzkts,ist->fzkis", back_im, sin_two_y, precision=EXACT
    )
    half_im = jnp.einsum("fzkts,ist->fzkis", back_re, sin_two_y, precision=EXACT) + jnp.einsum(
        "fzkts,ist->fzkis", back_im, cos_two_y, precision=EXACT
    )
    line_back_re = jnp.einsum("fzkis,js->fzkji", half_re, cos_one_y, precision=EXACT) - jnp.einsum(
        "fzkis,js->fzkji", half_im, sin_one_y, precision=EXACT
    )
    line_back_im = jnp.einsum("fzkis,js->fzkji", half_re, sin_one_y, precision=EXACT) + jnp.einsum(
        "fzkis,js->fzkji", half_im, cos_one_y, precision=EXACT
    )
    pencils_back = jnp.stack([line_back_re, line_back_im], axis=1).reshape(
        5, 2, depth_here, local, pen_size, rows_here
    )
    pencils_back = jnp.transpose(pencils_back, (0, 1, 2, 4, 3, 5)).reshape(
        5, 2, depth_here, pen_size, local * rows_here
    )
    fields = lax.all_to_all(pencils_back, "pen", split_axis=3, concat_axis=3, tiled=True)
    fields = fields.reshape(5, 2, levels, count, rows_here)
    wave_x = (jnp.arange(count, dtype=jnp.float32) * (2.0 * math.pi / length_x))[None, :, None]
    filter_u = fields[0]
    filter_v = fields[1]
    filter_w = fields[2]
    slope_uy = fields[3]
    slope_wy = fields[4]
    spin_hat = jnp.stack([-wave_x * filter_v[1] - slope_uy[0], wave_x * filter_v[0] - slope_uy[1]])
    slope_hat = jnp.stack([-wave_x * filter_w[1], wave_x * filter_w[0]])
    sixfold = jnp.stack([filter_u, filter_v, filter_w, spin_hat, slope_hat, slope_wy])
    factor = jnp.where(jnp.arange(count) == 0, 1.0, 2.0) / length_x
    sixfold = sixfold * factor[None, None, None, :, None]
    sixfold = jnp.pad(sixfold, ((0, 0), (0, 0), (0, 0), (0, blocks_x * RADIX_X - count), (0, 0)))
    sixfold = sixfold.reshape(6, 2, levels, blocks_x, RADIX_X, rows_here)
    six_re = sixfold[:, 0]
    six_im = sixfold[:, 1]
    mix_re = jnp.einsum("fzmky,ikm->fzyik", six_re, cos_two_x, precision=EXACT) - jnp.einsum(
        "fzmky,ikm->fzyik", six_im, sin_two_x, precision=EXACT
    )
    mix_im = jnp.einsum("fzmky,ikm->fzyik", six_re, sin_two_x, precision=EXACT) + jnp.einsum(
        "fzmky,ikm->fzyik", six_im, cos_two_x, precision=EXACT
    )
    physical = jnp.einsum("fzyik,jk->fzyji", mix_re, cos_one_x, precision=EXACT) - jnp.einsum(
        "fzyik,jk->fzyji", mix_im, sin_one_x, precision=EXACT
    )
    physical = physical.reshape(6, levels, rows_here, length_x)
    smooth_u = physical[0]
    smooth_v = physical[1]
    smooth_w = physical[2]
    spin_z = physical[3]
    w_slope_x = physical[4]
    w_slope_y = physical[5]
    spin_x = w_slope_y - slopes_z[1]
    spin_y = slopes_z[0] - w_slope_x
    row_count = sample_cell.shape[1]
    cells_flat = sample_cell.reshape(row_count, SAMP)
    weights = sample_weight.reshape(row_count, SAMP)
    picked = velocity[0].reshape(-1)[cells_flat]
    weighted = weights * picked
    owners = sample_turbine.reshape(row_count)
    turbines = thrust.shape[0]
    per_owner = turbines // pen_size
    owner_match = owners[:, None] == jnp.arange(turbines, dtype=jnp.int32)[None, :]
    onehot = owner_match.astype(jnp.float32)
    row_num = jnp.sum(weighted, axis=1)
    row_den = jnp.sum(weights, axis=1)
    part_num = jnp.dot(row_num, onehot, precision=EXACT)
    part_den = jnp.dot(row_den, onehot, precision=EXACT)
    recv_num, recv_den = (
        lax.all_to_all(
            part_num.reshape(pen_size, per_owner), "pen", split_axis=0, concat_axis=0, tiled=True
        ),
        lax.all_to_all(
            part_den.reshape(pen_size, per_owner), "pen", split_axis=0, concat_axis=0, tiled=True
        ),
    )
    own_num = jnp.sum(recv_num, axis=0)
    own_den = jnp.sum(recv_den, axis=0)
    own_num, own_den = lax.psum((own_num, own_den), "gz")
    own_thrust = lax.dynamic_slice_in_dim(thrust, lax.axis_index("pen") * per_owner, per_owner)
    own_speed = own_num / own_den
    own_force = -0.5 * own_thrust * own_speed * jnp.abs(own_speed)
    disk_force = lax.all_gather(own_force, "pen", axis=0, tiled=True)
    row_force = jnp.dot(onehot, disk_force, precision=EXACT)
    cell_force = (row_force[:, None] * weights).reshape(-1)
    push_x = (
        jnp.zeros((levels * rows_here * length_x,), jnp.float32)
        .at[cells_flat.reshape(-1)]
        .add(cell_force)
    )
    push_x = push_x.reshape(levels, rows_here, length_x)
    tendency = jnp.stack(
        [
            smooth_v * spin_z - smooth_w * spin_y + push_x,
            smooth_w * spin_x - smooth_u * spin_z,
            smooth_u * spin_y - smooth_v * spin_x,
        ]
    )
    velocity_next = velocity + SECTION * tendency
    return (tendency, velocity_next)


LANES = 128
RADIX = 16


def rfft_parts(xs):
    n = len(xs)
    if n == 2:
        return [(xs[0] + xs[1], None), (xs[0] - xs[1], None)]
    even, odd = rfft_parts(xs[0::2]), rfft_parts(xs[1::2])
    out = [None] * (n // 2 + 1)
    out[0] = (even[0][0] + odd[0][0], None)
    out[n // 2] = (even[0][0] - odd[0][0], None)
    out[n // 4] = (even[n // 4][0], -odd[n // 4][0])
    for r in range(1, n // 4):
        (er, ei), (pr, pi) = even[r], odd[r]
        c, s = math.cos(2 * math.pi * r / n), math.sin(2 * math.pi * r / n)
        if 8 * r == n:
            tr, ti = (pr + pi) * c, (pi - pr) * c
        else:
            tr, ti = pr * c + pi * s, pi * c - pr * s
        out[r] = (er + tr, ei + ti)
        out[n // 2 - r] = (er - tr, ti - ei)
    return out


def irfft_parts(spec):
    n = 2 * (len(spec) - 1)
    if n == 2:
        return [spec[0][0] + spec[1][0], spec[0][0] - spec[1][0]]
    even, odd = [None] * (n // 4 + 1), [None] * (n // 4 + 1)
    even[0] = (spec[0][0] + spec[n // 2][0], None)
    odd[0] = (spec[0][0] - spec[n // 2][0], None)
    mid_re, mid_im = spec[n // 4]
    even[n // 4] = (2.0 * mid_re, None)
    odd[n // 4] = (-2.0 * mid_im, None)
    for r in range(1, n // 4):
        (ar, ai), (br, bi) = spec[r], spec[n // 2 - r]
        c, s = math.cos(2 * math.pi * r / n), math.sin(2 * math.pi * r / n)
        even[r] = (ar + br, ai - bi)
        dr, di = ar - br, ai + bi
        if 8 * r == n:
            odd[r] = ((dr - di) * c, (dr + di) * c)
        else:
            odd[r] = (dr * c - di * s, dr * s + di * c)
    out = [None] * n
    out[0::2] = irfft_parts(even)
    out[1::2] = irfft_parts(odd)
    return out


def halves(x):
    hi = x.astype(jnp.bfloat16)
    return hi, (x - hi.astype(jnp.float32)).astype(jnp.bfloat16)


def np_halves(x):
    x = np.asarray(x, np.float64)
    hi = x.astype(jnp.bfloat16)
    return hi, (x - hi.astype(np.float64)).astype(jnp.bfloat16)


class Plan:
    def __init__(self, length_x, length_y):
        modes = (length_x - 1) // 3 + 1
        self.length_x, self.length_y = length_x, length_y
        self.base = modes // RADIX
        self.longer = modes - RADIX * self.base
        self.width = 2 * self.base

    def lanes(self, residue):
        places = []
        for m in range(self.base + 1):
            k = residue + RADIX * m
            if 3 * k < self.length_x:
                if m < self.base:
                    places += [(m, k, 0), (self.base + m, k, 1)]
                else:
                    places += [(self.width, k, 0), (self.width + 1, k, 1)]
        return places

    def x_weights(self):
        i = np.arange(LANES, dtype=np.int64)
        out = np.zeros((RADIX // 2, 2 * LANES, 2 * LANES))
        for pair in range(RADIX // 2):
            partner = RADIX - pair if pair else RADIX // 2
            for half, residue in enumerate((pair, partner)):
                for lane, k, imag in self.lanes(residue):
                    phase = 2 * np.pi * ((i * k) % self.length_x) / self.length_x
                    c, s = np.cos(phase), np.sin(phase)
                    on_re, on_im = ((-s, c) if imag else (c, s))
                    column = out[pair, :, half * LANES + lane]
                    if pair == 0:
                        column[half * LANES:(half + 1) * LANES] = on_re
                    else:
                        column[:LANES] = on_re
                        column[LANES:] = -on_im if half else on_im
        return out

    def wave_lanes(self):
        out = np.zeros((RADIX, LANES), np.float32)
        for residue in range(RADIX):
            for lane, k, imag in self.lanes(residue):
                out[residue, lane] = (2 * np.pi * k / self.length_x) * (1 if imag else -1)
        return out

    def y_weights(self, rows):
        signed = np.arange(self.length_y)
        signed = np.where(signed <= self.length_y // 2, signed, signed - self.length_y)
        signed = signed[3 * np.abs(signed) < self.length_y]
        gap = np.arange(rows)[:, None] - np.arange(rows)[None, :]
        out = np.zeros((RADIX // 2, 4 * rows, 2 * rows))
        scale = 1.0 / (self.length_x * self.length_y)
        for pair in range(RADIX // 2):
            for op in range(2):
                blocks = []
                for residue in ((pair,) if pair else (0, RADIX // 2)):
                    chosen = signed[(signed - residue) % RADIX == 0]
                    phase = 2 * np.pi * ((gap[:, :, None] * chosen) % self.length_y) / self.length_y
                    kernel = np.exp(1j * phase)
                    if op:
                        kernel = kernel * (1j * 2 * np.pi * chosen / self.length_y)
                    blocks.append(kernel.sum(-1) * scale)
                base = 2 * rows * op
                if pair:
                    p = blocks[0]
                    full = np.block([[p.real, -p.imag], [p.imag, p.real]])
                else:
                    zero = np.zeros((rows, rows))
                    full = np.block([[blocks[0].real, zero], [zero, blocks[1].real]])
                out[pair, base:base + 2 * rows] = full
        return out


def triple(lhs_hi, lhs_lo, rhs_hi, rhs_lo, dims):
    def product(a, b):
        return lax.dot_general(a, b, (dims, ((), ())), preferred_element_type=jnp.float32)

    return product(lhs_hi, rhs_hi) + (product(lhs_hi, rhs_lo) + product(lhs_lo, rhs_hi))


def pair_place(residue):
    if residue == 0 or residue == RADIX // 2:
        return 0, (1 if residue else 0)
    return (residue, 0) if residue < RADIX // 2 else (RADIX - residue, 1)


def x_forward_kernel(plan, rows, vel_ref, whi_ref, wlo_ref, out_ref, ahi, alo, spec):
    comps = vel_ref.shape[0]
    step = 16

    def butterflies(g, carry):
        c = g // (rows // step)
        at = pl.multiple_of((g % (rows // step)) * step, step)
        block = [vel_ref[c, 0, pl.ds(at, step), j * LANES:(j + 1) * LANES] for j in range(RADIX)]
        parts = rfft_parts(block)
        row = pl.multiple_of(g * step, step)
        for pair in range(RADIX // 2):
            both = (parts[0][0], parts[RADIX // 2][0]) if pair == 0 else parts[pair]
            for half in range(2):
                hi, lo = halves(both[half])
                ahi[pair, pl.ds(row, step), half * LANES:(half + 1) * LANES] = hi
                alo[pair, pl.ds(row, step), half * LANES:(half + 1) * LANES] = lo
        return carry

    lax.fori_loop(0, comps * rows // step, butterflies, 0)

    def multiply(pair, carry):
        spec[pair] = triple(ahi[pair], alo[pair], whi_ref[pair], wlo_ref[pair], ((1,), (0,)))
        return carry

    lax.fori_loop(0, RADIX // 2, multiply, 0)
    width, longer = plan.width, plan.longer

    def pack(g, carry):
        at = pl.multiple_of(g * 8, 8)
        lane = lax.broadcasted_iota(jnp.int32, (8, LANES), 1)

        def tile(c, residue):
            pair, half = pair_place(residue)
            return spec[pair, pl.ds(c * rows + at, 8), half * LANES:(half + 1) * LANES]

        def turned(x, shift):
            return pltpu.roll(x, shift % LANES, 1)

        w_at = 2 * width - LANES
        for p in range(RADIX):
            u, v, w = tile(0, p), tile(1, p), tile(2, p)
            if p == 0:
                last = tile(0, longer - 1)
                u = jnp.where(lane == plan.base, turned(last, plan.base - width), u)
                w = jnp.where(lane == plan.base, turned(last, plan.base - width - 1), w)
            moved_u = turned(u, width)
            first = jnp.where(lane < width, v, moved_u)
            second = jnp.where(lane < w_at, moved_u, turned(w, w_at))
            if p < longer:
                slot_b = turned(v, LANES - 2 - width)
            else:
                slot_a = turned(tile(0, p - longer + RADIX - longer), LANES - 4 - width)
                second = jnp.where(lane >= LANES - 4, slot_a, second)
                slot_b = turned(tile(0, p - longer), LANES - 2 - width)
            second = jnp.where(lane >= LANES - 2, slot_b, second)
            out_ref[p, pl.ds(at, 8), :] = first
            out_ref[p, pl.ds(rows + at, 8), :] = second
        return carry

    lax.fori_loop(0, rows // 8, pack, 0)


def y_kernel(plan, rows, in_ref, qhi_ref, qlo_ref, out_ref, ahi, alo, spec):
    step = 16

    def butterflies(g, carry):
        tile_index = g // (rows // step)
        at = pl.multiple_of((g % (rows // step)) * step, step)
        src = pl.multiple_of(g * step, step)
        parts = rfft_parts([in_ref[s, pl.ds(src, step), :] for s in range(RADIX)])
        for pair in range(RADIX // 2):
            both = (parts[0][0], parts[RADIX // 2][0]) if pair == 0 else parts[pair]
            for half in range(2):
                hi, lo = halves(both[half])
                ahi[tile_index, pair, pl.ds(half * rows + at, step), :] = hi
                alo[tile_index, pair, pl.ds(half * rows + at, step), :] = lo
        return carry

    lax.fori_loop(0, 2 * rows // step, butterflies, 0)

    def multiply(pair, carry):
        hi = jnp.concatenate([ahi[0, pair], ahi[1, pair]], axis=1)
        lo = jnp.concatenate([alo[0, pair], alo[1, pair]], axis=1)
        spec[pair] = triple(qhi_ref[pair], qlo_ref[pair], hi, lo, ((1,), (0,)))
        return carry

    lax.fori_loop(0, RADIX // 2, multiply, 0)
    width = plan.width

    def back(op, tile_index, at):
        cols = slice(tile_index * LANES, (tile_index + 1) * LANES)

        def part(pair, half):
            return spec[pair, pl.ds((2 * op + half) * rows + at, 8), cols]

        lines = [(part(0, 0), None)]
        lines += [(part(pair, 0), part(pair, 1)) for pair in range(1, RADIX // 2)]
        lines += [(part(0, 1), None)]
        return irfft_parts(lines)

    def finish(g, carry):
        at = pl.multiple_of(g * 8, 8)
        for block, (op, tile_index) in enumerate(((0, 0), (0, 1), (1, 1))):
            for s, value in enumerate(back(op, tile_index, at)):
                out_ref[s, pl.ds(block * rows + at, 8), :] = value
        return carry

    lax.fori_loop(0, rows // 8, finish, 0)

    def finish_half(g, carry):
        at = pl.multiple_of(g * 8, 8)
        lane = lax.broadcasted_iota(jnp.int32, (8, LANES), 1)
        upper, lower = back(1, 0, at), back(1, 0, at + rows // 2)
        for s in range(RADIX):
            both = jnp.where(lane >= width, upper[s], pltpu.roll(lower[s], LANES // 2, 1))
            out_ref[s, pl.ds(3 * rows + at, 8), :] = both
        return carry

    lax.fori_loop(0, rows // 16, finish_half, 0)


def x_back_kernel(
    plan, rows, slope_ref, in_ref, whi_ref, wlo_ref, wave_ref, vel_ref, rim_ref, push_ref,
    tend_ref, next_ref, lhi, llo, spec, phys,
):
    width, longer, base = plan.width, plan.longer, plan.base
    step = 16
    w_at = 2 * width - LANES

    def unpack(g, carry):
        at = pl.multiple_of(g * step, step)
        lane = lax.broadcasted_iota(jnp.int32, (step, LANES), 1)
        upper = g < rows // 2 // step
        half_at = pl.multiple_of((g % (rows // 2 // step)) * step, step)

        def turned(x, shift):
            return pltpu.roll(x, shift % LANES, 1)

        def first(p, op):
            if op == 0:
                return in_ref[p, pl.ds(at, step), :]
            both = in_ref[p, pl.ds(3 * rows + half_at, step), :]
            return jnp.where(upper, both, turned(both, LANES // 2))

        def second(p, op):
            return in_ref[p, pl.ds((1 + op) * rows + at, step), :]

        def w_tile(p, op):
            return turned(second(p, op), -w_at)

        def v_tile(p):
            tile = first(p, 0)
            if p < longer:
                tile = jnp.where(lane >= width, turned(second(p, 0), width + 2 - LANES), tile)
            return tile

        def u_base(p, op):
            return turned(jnp.where(lane >= width, first(p, op), second(p, op)), -width)

        def u_tile(p, op):
            tile = u_base(p, op)
            if p < RADIX - longer:
                extra = turned(second(p + longer, op), width + 2 - LANES)
            elif p < 2 * (RADIX - longer):
                extra = turned(second(p + longer - RADIX + longer, op), width + 4 - LANES)
            elif p == longer - 1:
                extra = jnp.where(
                    lane == width,
                    turned(u_base(0, op), width - base),
                    turned(w_tile(0, op), width + 1 - base),
                )
            else:
                return tile
            return jnp.where(lane >= width, extra, tile)

        def slope(tile, p):
            forward, backward = turned(tile, -base), turned(tile, base)
            swapped = jnp.where(lane < base, forward, backward)
            last = jnp.where(lane == width, turned(tile, -1), turned(tile, 1))
            return jnp.where(lane < width, swapped, last) * wave_ref[pl.ds(p, 1), :]

        for p in range(RADIX):
            u, v, w = u_tile(p, 0), v_tile(p), w_tile(p, 0)
            uy, wy = u_tile(p, 1), w_tile(p, 1)
            fields = [u, v, w, slope(v, p) - uy, slope(w, p), wy]
            pair, half = pair_place(p)
            for f, value in enumerate(fields):
                if pair == 0:
                    value = value * (2.0 if half else jnp.where(lane == 0, 1.0, 2.0))
                hi, lo = halves(value)
                row = pl.multiple_of(f * rows + at, step)
                lhi[pair, pl.ds(row, step), half * LANES:(half + 1) * LANES] = hi
                llo[pair, pl.ds(row, step), half * LANES:(half + 1) * LANES] = lo
        return carry

    lax.fori_loop(0, rows // step, unpack, 0)

    def multiply(pair, carry):
        spec[pair] = triple(lhi[pair], llo[pair], whi_ref[pair], wlo_ref[pair], ((1,), (1,)))
        return carry

    lax.fori_loop(0, RADIX // 2, multiply, 0)
    z_scale = slope_ref[0]

    def finish(g, carry):
        at = pl.multiple_of(g * 8, 8)
        for f in range(6):
            def part(pair, half):
                return spec[pair, pl.ds(f * rows + at, 8), half * LANES:(half + 1) * LANES]

            lines = [(part(0, 0), None)]
            lines += [(part(pair, 0), part(pair, 1)) for pair in range(1, RADIX // 2)]
            lines += [(part(0, 1), None)]
            for j, value in enumerate(irfft_parts(lines)):
                phys[f, :, j * LANES:(j + 1) * LANES] = value
        for j in range(RADIX):
            cols = slice(j * LANES, (j + 1) * LANES)
            u, v, w, spin_z, w_x, w_y = [phys[f, :, cols] for f in range(6)]
            push = push_ref[j // 2, pl.ds(at, 8), (j % 2) * LANES:(j % 2 + 1) * LANES]
            spin_x = w_y - z_scale * rim_ref[1, 0, pl.ds(at, 8), cols]
            spin_y = z_scale * rim_ref[0, 0, pl.ds(at, 8), cols] - w_x
            rates = (v * spin_z - w * spin_y + push, w * spin_x - u * spin_z, u * spin_y - v * spin_x)
            for c, rate in enumerate(rates):
                tend_ref[c, 0, pl.ds(at, 8), cols] = rate
                next_ref[c, 0, pl.ds(at, 8), cols] = vel_ref[c, 0, pl.ds(at, 8), cols] + SECTION * rate
        return carry

    lax.fori_loop(0, rows // 8, finish, 0)


def cell_codes(cell, length_x):
    blocks = length_x // (2 * LANES)
    row, column = cell // length_x, cell % length_x
    return row, column // (2 * LANES), column % (2 * LANES), blocks


def sums_kernel(rows, vel_ref, cell_ref, owner_ref, weight_ref, out_ref, table_hi, table_lo, high, low, picked):
    length_x = vel_ref.shape[-1]
    blocks = length_x // (2 * LANES)
    for b in range(blocks):
        block = vel_ref[0, 0, :, b * 2 * LANES:(b + 1) * 2 * LANES]
        hi, lo = halves(block.T)
        table_hi[:, b * rows:(b + 1) * rows] = hi
        table_lo[:, b * rows:(b + 1) * rows] = lo
    row, block, lane_code, _ = cell_codes(cell_ref[0], length_x)
    high[...] = block * rows + row
    low[...] = lane_code
    cells = blocks * rows

    def gather(i, carry):
        h = jnp.concatenate([high[pl.ds(2 * i, 1), :], high[pl.ds(2 * i + 1, 1), :]], axis=1)
        l = jnp.concatenate([low[pl.ds(2 * i, 1), :], low[pl.ds(2 * i + 1, 1), :]], axis=1)
        hot = (lax.broadcasted_iota(jnp.int32, (cells, 2 * LANES), 0) == h).astype(jnp.float32).astype(jnp.bfloat16)
        found = jnp.dot(table_hi[...], hot, preferred_element_type=jnp.float32)
        found += jnp.dot(table_lo[...], hot, preferred_element_type=jnp.float32)
        mine = lax.broadcasted_iota(jnp.int32, (2 * LANES, 2 * LANES), 0) == l
        value = jnp.sum(jnp.where(mine, found, 0.0), axis=0, keepdims=True)
        picked[pl.ds(2 * i, 1), :] = value[:, :LANES]
        picked[pl.ds(2 * i + 1, 1), :] = value[:, LANES:]
        return carry

    lax.fori_loop(0, cell_ref.shape[1] // 2, gather, 0)
    weights = weight_ref[0]
    row_num = jnp.sum(weights * picked[...], axis=1, keepdims=True)
    row_den = jnp.sum(weights, axis=1, keepdims=True)
    mine = lax.broadcasted_iota(jnp.int32, weights.shape, 1) == owner_ref[0]
    num = jnp.sum(jnp.where(mine, row_num, 0.0), axis=0, keepdims=True)
    den = jnp.sum(jnp.where(mine, row_den, 0.0), axis=0, keepdims=True)
    out_ref[...] = jnp.concatenate([num, den, jnp.zeros((6, LANES), jnp.float32)], axis=0)


def push_kernel(rows, length_x, sum_ref, thrust_ref, cell_ref, owner_ref, weight_ref, out_ref, high, low, c_hi, c_lo, acc):
    blocks = length_x // (2 * LANES)
    cells = blocks * rows
    turbines = thrust_ref.shape[1]
    total = jnp.sum(sum_ref[...], axis=0)
    speed = total[0:1, :turbines] / total[1:2, :turbines]
    force = -0.5 * thrust_ref[...] * speed * jnp.abs(speed)
    mine = lax.broadcasted_iota(jnp.int32, (cell_ref.shape[1], turbines), 1) == owner_ref[0]
    row_force = jnp.sum(jnp.where(mine, force, 0.0), axis=1, keepdims=True)
    cell_force = row_force * weight_ref[0]
    big = cell_force.astype(jnp.bfloat16).astype(jnp.float32)
    c_hi[...] = big
    c_lo[...] = cell_force - big
    row, block, lane_code, _ = cell_codes(cell_ref[0], length_x)
    high[...] = block * rows + row
    low[...] = lane_code
    acc[...] = jnp.zeros_like(acc)

    def scatter(i, carry):
        def two(ref):
            return jnp.concatenate([ref[pl.ds(2 * i, 1), :], ref[pl.ds(2 * i + 1, 1), :]], axis=1)

        hot = (lax.broadcasted_iota(jnp.int32, (cells, 2 * LANES), 0) == two(high)).astype(jnp.float32).astype(jnp.bfloat16)
        mine = lax.broadcasted_iota(jnp.int32, (2 * LANES, 2 * LANES), 0) == two(low)
        upper = jnp.where(mine, two(c_hi), 0.0).astype(jnp.bfloat16)
        lower = jnp.where(mine, two(c_lo), 0.0).astype(jnp.bfloat16)
        dims = (((1,), (1,)), ((), ()))
        acc[...] += lax.dot_general(hot, upper, dims, preferred_element_type=jnp.float32) + lax.dot_general(
            hot, lower, dims, preferred_element_type=jnp.float32
        )
        return carry

    lax.fori_loop(0, cell_ref.shape[1] // 2, scatter, 0)
    for b in range(blocks):
        out_ref[b] = acc[b * rows:(b + 1) * rows, :]


def fits(velocity, sample_cell, thrust, pen_size):
    _, levels, rows, length_x = velocity.shape
    plan = Plan(length_x, rows * pen_size)
    return (
        pen_size == RADIX
        and levels == 1
        and 2 * rows == LANES
        and length_x == RADIX * LANES
        and sample_cell.shape[2] == LANES
        and sample_cell.shape[1] % 8 == 0
        and thrust.shape[0] <= LANES
        and 3 * plan.width + 4 == 2 * LANES
        and 2 * (RADIX - plan.longer) == plan.longer - 1
    )


def packed_shards(velocity, inv_span, sample_cell, sample_turbine, sample_weight, thrust):
    comps, _, rows, length_x = velocity.shape
    pen_size = lax.axis_size("pen")
    plan = Plan(length_x, rows * pen_size)
    f32, bf16 = jnp.float32, jnp.bfloat16
    half = RADIX // 2
    wide = 2 * LANES
    w_hi, w_lo = [jnp.asarray(x) for x in np_halves(plan.x_weights())]
    q_hi, q_lo = [jnp.asarray(x) for x in np_halves(plan.y_weights(rows))]
    waves = jnp.asarray(plan.wave_lanes())
    shape = jax.ShapeDtypeStruct
    vmem = pltpu.VMEM

    packed = pl.pallas_call(
        functools.partial(x_forward_kernel, plan, rows),
        out_shape=shape((RADIX, 2 * rows, LANES), f32),
        scratch_shapes=[
            vmem((half, comps * rows, wide), bf16),
            vmem((half, comps * rows, wide), bf16),
            vmem((half, comps * rows, wide), f32),
        ],
        name="x_forward",
    )(velocity, w_hi, w_lo)
    columns = lax.all_to_all(packed, "pen", split_axis=0, concat_axis=0, tiled=True)

    samples = sample_cell.shape[1]
    sample_scratch = [vmem((samples, LANES), jnp.int32)] * 2
    part = pl.pallas_call(
        functools.partial(sums_kernel, rows),
        out_shape=shape((8, LANES), f32),
        grid=(1,),
        in_specs=[
            pl.BlockSpec((1, 1, rows, length_x), lambda i: (0, 0, 0, 0)),
            pl.BlockSpec(sample_cell.shape, lambda i: (0, 0, 0)),
            pl.BlockSpec(sample_turbine.shape, lambda i: (0, 0, 0)),
            pl.BlockSpec(sample_weight.shape, lambda i: (0, 0, 0)),
        ],
        out_specs=pl.BlockSpec((8, LANES), lambda i: (0, 0)),
        scratch_shapes=[vmem((wide, length_x * rows // wide), bf16)] * 2
        + sample_scratch
        + [vmem((samples, LANES), f32)],
        name="disk_sums",
    )(velocity, sample_cell, sample_turbine, sample_weight)

    if lax.axis_size("gz") == 2:
        swap = [(0, 1), (1, 0)]
        rims = lax.ppermute(velocity[:2], "gz", swap)
        sign = 1.0 - 2.0 * lax.axis_index("gz").astype(f32)
        part = part + lax.ppermute(part, "gz", swap)
        scale = sign * inv_span
    else:
        around = padded(velocity[:2], (("gz", 1),), 1)
        rims = around[:, 2:] - around[:, :-2]
        part = lax.psum(part, "gz")
        scale = inv_span
    parts = lax.all_to_all(
        jnp.broadcast_to(part[None], (pen_size, 8, LANES)), "pen", split_axis=0, concat_axis=0, tiled=True
    )
    push = pl.pallas_call(
        functools.partial(push_kernel, rows, length_x),
        out_shape=shape((length_x // wide, rows, wide), f32),
        scratch_shapes=sample_scratch
        + [vmem((samples, LANES), f32)] * 2
        + [vmem((length_x * rows // wide, wide), f32)],
        name="disk_push",
    )(parts, thrust[None], sample_cell, sample_turbine, sample_weight)

    answers = pl.pallas_call(
        functools.partial(y_kernel, plan, rows),
        out_shape=shape((RADIX, 3 * rows + rows // 2, LANES), f32),
        scratch_shapes=[
            vmem((2, half, 2 * rows, LANES), bf16),
            vmem((2, half, 2 * rows, LANES), bf16),
            vmem((half, 4 * rows, wide), f32),
        ],
        name="y_operators",
    )(columns, q_hi, q_lo)
    fields = lax.all_to_all(answers, "pen", split_axis=0, concat_axis=0, tiled=True)

    out = shape(velocity.shape, f32)
    whole = pl.BlockSpec(memory_space=pltpu.VMEM)
    return pl.pallas_call(
        functools.partial(x_back_kernel, plan, rows),
        out_shape=(out, out),
        in_specs=[pl.BlockSpec(memory_space=pltpu.SMEM)] + [whole] * 7,
        out_specs=(whole, whole),
        scratch_shapes=[
            vmem((half, 6 * rows, wide), bf16),
            vmem((half, 6 * rows, wide), bf16),
            vmem((half, 6 * rows, wide), f32),
            vmem((6, 8, length_x), f32),
        ],
        name="x_back",
    )(scale, fields, w_hi, w_lo, waves, velocity, rims, push)


def program(*arguments):
    velocity, sample_cell, thrust = arguments[0], arguments[2], arguments[5]
    if fits(velocity, sample_cell, thrust, lax.axis_size("pen")):
        return packed_shards(*arguments)
    return shards(*arguments)


def solution(mesh):
    return jax.shard_map(
        program,
        mesh=mesh,
        in_specs=(
            P(None, "gz", "pen", None),
            P("gz"),
            P("gz", "pen", None),
            P("gz", "pen", None),
            P("gz", "pen", None),
            P(),
        ),
        out_specs=(P(None, "gz", "pen", None), P(None, "gz", "pen", None)),
        check_vma=False,
    )
```

```python
import functools
import math

import jax
import jax.numpy as jnp
import numpy as np
from jax import lax
from jax.experimental import pallas as pl
from jax.experimental.pallas import tpu as pltpu
from jax.sharding import PartitionSpec as P

SAMP = 128


SECTION = 0.1
EXACT = lax.Precision.HIGHEST
RADIX_X = 64
RADIX_Y = 32


def padded(value, sides, width):
    for axis, dim in sides:
        size, length = (lax.axis_size(axis), value.shape[dim])
        up = [(i, (i + 1) % size) for i in range(size - 1)]
        down = [(j, i) for i, j in up]
        last = lax.slice_in_dim(value, length - width, length, axis=dim)
        first = lax.slice_in_dim(value, 0, width, axis=dim)
        before = lax.ppermute(last, axis, up)
        after = lax.ppermute(first, axis, down)
        value = jnp.concatenate([before, value, after], axis=dim)
    return value


def pair_table(first_index, second_index, length):
    angles = (first_index * second_index % length).astype(jnp.float32) * (2.0 * math.pi / length)
    return (jnp.cos(angles), jnp.sin(angles))


def shards(velocity, inv_span, sample_cell, sample_turbine, sample_weight, thrust):
    components, levels, rows_here, length_x = velocity.shape
    pen_size = lax.axis_size("pen")
    length_y = rows_here * pen_size
    top_y = (length_y - 1) // 3
    width_y = (2 * top_y + 128) // 128 * 128
    count = -(-((length_x - 1) // 3 + 1) // pen_size) * pen_size
    local = count // pen_size
    inner_x = length_x // RADIX_X
    blocks_x = -(-count // RADIX_X)
    cos_one_x, sin_one_x = pair_table(
        jnp.arange(RADIX_X, dtype=jnp.int32)[:, None],
        jnp.arange(RADIX_X, dtype=jnp.int32)[None, :],
        RADIX_X,
    )
    wave_slots = (
        jnp.arange(RADIX_X, dtype=jnp.int32)[None, :, None]
        + RADIX_X * jnp.arange(blocks_x, dtype=jnp.int32)[None, None, :]
    )
    cos_two_x, sin_two_x = pair_table(
        jnp.arange(inner_x, dtype=jnp.int32)[:, None, None], wave_slots, length_x
    )
    inner_y = length_y // RADIX_Y
    blocks_y = -(-width_y // RADIX_Y)
    cos_one_y, sin_one_y = pair_table(
        jnp.arange(RADIX_Y, dtype=jnp.int32)[:, None],
        jnp.arange(RADIX_Y, dtype=jnp.int32)[None, :] - top_y,
        RADIX_Y,
    )
    slot_grid = (
        jnp.arange(RADIX_Y, dtype=jnp.int32)[None, :, None]
        + RADIX_Y * jnp.arange(blocks_y, dtype=jnp.int32)[None, None, :]
    )
    usable = (slot_grid <= 2 * top_y).astype(jnp.float32)
    cos_two_y, sin_two_y = pair_table(
        jnp.arange(inner_y, dtype=jnp.int32)[:, None, None], slot_grid - top_y, length_y
    )
    cos_two_y = cos_two_y * usable
    sin_two_y = sin_two_y * usable
    wave_y = (jnp.arange(width_y, dtype=jnp.int32) - top_y).astype(jnp.float32) * (
        2.0 * math.pi / length_y
    )
    first_mode = lax.axis_index("pen") * local
    kept_x = (3 * (first_mode + jnp.arange(local, dtype=jnp.int32)) < length_x).astype(jnp.float32)
    rims = padded(velocity[:2], (("gz", 1),), 1)
    slopes_z = (rims[:, 2:] - rims[:, :-2]) * inv_span[None, :, None, None]
    folded = velocity.reshape(components, levels, rows_here, RADIX_X, inner_x)
    section_re = jnp.einsum("czyji,jk->czyik", folded, cos_one_x, precision=EXACT)
    section_im = -jnp.einsum("czyji,jk->czyik", folded, sin_one_x, precision=EXACT)
    four_re = jnp.einsum("czyik,ikm->czymk", section_re, cos_two_x, precision=EXACT) + jnp.einsum(
        "czyik,ikm->czymk", section_im, sin_two_x, precision=EXACT
    )
    four_im = jnp.einsum("czyik,ikm->czymk", section_im, cos_two_x, precision=EXACT) - jnp.einsum(
        "czyik,ikm->czymk", section_re, sin_two_x, precision=EXACT
    )
    spectra = jnp.stack([four_re, four_im], axis=1).reshape(
        components, 2, levels, rows_here, blocks_x * RADIX_X
    )
    spectra = jnp.transpose(spectra[..., :count], (0, 1, 2, 4, 3))
    spectra = spectra.reshape(components, 2, levels, 1, count * rows_here)
    pencil_block = lax.all_to_all(spectra, "pen", split_axis=4, concat_axis=3, tiled=True)
    depth_here = pencil_block.shape[2]
    pencils = pencil_block.reshape(components, 2, depth_here, pen_size, local, rows_here)
    lines = jnp.transpose(pencils, (0, 1, 2, 4, 3, 5)).reshape(
        components, 2, depth_here, local, RADIX_Y, inner_y
    )
    line_re = lines[:, 0]
    line_im = lines[:, 1]
    part_re = jnp.einsum("czkji,js->czkis", line_re, cos_one_y, precision=EXACT) + jnp.einsum(
        "czkji,js->czkis", line_im, sin_one_y, precision=EXACT
    )
    part_im = jnp.einsum("czkji,js->czkis", line_im, cos_one_y, precision=EXACT) - jnp.einsum(
        "czkji,js->czkis", line_re, sin_one_y, precision=EXACT
    )
    mode_re = jnp.einsum("czkis,ist->czkts", part_re, cos_two_y, precision=EXACT) + jnp.einsum(
        "czkis,ist->czkts", part_im, sin_two_y, precision=EXACT
    )
    mode_im = jnp.einsum("czkis,ist->czkts", part_im, cos_two_y, precision=EXACT) - jnp.einsum(
        "czkis,ist->czkts", part_re, sin_two_y, precision=EXACT
    )
    mode_values = jnp.stack([mode_re, mode_im], axis=1).reshape(
        components, 2, depth_here, local, blocks_y * RADIX_Y
    )
    mode_values = mode_values * kept_x[None, None, None, :, None]
    paired = jnp.stack([mode_values[0], mode_values[2]])
    slopes = jnp.stack([-wave_y * paired[:, 1], wave_y * paired[:, 0]], axis=1)
    stacked = jnp.concatenate([mode_values, slopes], axis=0) * (1.0 / length_y)
    stacked = stacked.reshape(5, 2, depth_here, local, blocks_y, RADIX_Y)
    back_re = stacked[:, 0]
    back_im = stacked[:, 1]
    half_re = jnp.einsum("fzkts,ist->fzkis", back_re, cos_two_y, precision=EXACT) - jnp.einsum(
        "fzkts,ist->fzkis", back_im, sin_two_y, precision=EXACT
    )
    half_im = jnp.einsum("fzkts,ist->fzkis", back_re, sin_two_y, precision=EXACT) + jnp.einsum(
        "fzkts,ist->fzkis", back_im, cos_two_y, precision=EXACT
    )
    line_back_re = jnp.einsum("fzkis,js->fzkji", half_re, cos_one_y, precision=EXACT) - jnp.einsum(
        "fzkis,js->fzkji", half_im, sin_one_y, precision=EXACT
    )
    line_back_im = jnp.einsum("fzkis,js->fzkji", half_re, sin_one_y, precision=EXACT) + jnp.einsum(
        "fzkis,js->fzkji", half_im, cos_one_y, precision=EXACT
    )
    pencils_back = jnp.stack([line_back_re, line_back_im], axis=1).reshape(
        5, 2, depth_here, local, pen_size, rows_here
    )
    pencils_back = jnp.transpose(pencils_back, (0, 1, 2, 4, 3, 5)).reshape(
        5, 2, depth_here, pen_size, local * rows_here
    )
    fields = lax.all_to_all(pencils_back, "pen", split_axis=3, concat_axis=3, tiled=True)
    fields = fields.reshape(5, 2, levels, count, rows_here)
    wave_x = (jnp.arange(count, dtype=jnp.float32) * (2.0 * math.pi / length_x))[None, :, None]
    filter_u = fields[0]
    filter_v = fields[1]
    filter_w = fields[2]
    slope_uy = fields[3]
    slope_wy = fields[4]
    spin_hat = jnp.stack([-wave_x * filter_v[1] - slope_uy[0], wave_x * filter_v[0] - slope_uy[1]])
    slope_hat = jnp.stack([-wave_x * filter_w[1], wave_x * filter_w[0]])
    sixfold = jnp.stack([filter_u, filter_v, filter_w, spin_hat, slope_hat, slope_wy])
    factor = jnp.where(jnp.arange(count) == 0, 1.0, 2.0) / length_x
    sixfold = sixfold * factor[None, None, None, :, None]
    sixfold = jnp.pad(sixfold, ((0, 0), (0, 0), (0, 0), (0, blocks_x * RADIX_X - count), (0, 0)))
    sixfold = sixfold.reshape(6, 2, levels, blocks_x, RADIX_X, rows_here)
    six_re = sixfold[:, 0]
    six_im = sixfold[:, 1]
    mix_re = jnp.einsum("fzmky,ikm->fzyik", six_re, cos_two_x, precision=EXACT) - jnp.einsum(
        "fzmky,ikm->fzyik", six_im, sin_two_x, precision=EXACT
    )
    mix_im = jnp.einsum("fzmky,ikm->fzyik", six_re, sin_two_x, precision=EXACT) + jnp.einsum(
        "fzmky,ikm->fzyik", six_im, cos_two_x, precision=EXACT
    )
    physical = jnp.einsum("fzyik,jk->fzyji", mix_re, cos_one_x, precision=EXACT) - jnp.einsum(
        "fzyik,jk->fzyji", mix_im, sin_one_x, precision=EXACT
    )
    physical = physical.reshape(6, levels, rows_here, length_x)
    smooth_u = physical[0]
    smooth_v = physical[1]
    smooth_w = physical[2]
    spin_z = physical[3]
    w_slope_x = physical[4]
    w_slope_y = physical[5]
    spin_x = w_slope_y - slopes_z[1]
    spin_y = slopes_z[0] - w_slope_x
    row_count = sample_cell.shape[1]
    cells_flat = sample_cell.reshape(row_count, SAMP)
    weights = sample_weight.reshape(row_count, SAMP)
    picked = velocity[0].reshape(-1)[cells_flat]
    weighted = weights * picked
    owners = sample_turbine.reshape(row_count)
    turbines = thrust.shape[0]
    per_owner = turbines // pen_size
    owner_match = owners[:, None] == jnp.arange(turbines, dtype=jnp.int32)[None, :]
    onehot = owner_match.astype(jnp.float32)
    row_num = jnp.sum(weighted, axis=1)
    row_den = jnp.sum(weights, axis=1)
    part_num = jnp.dot(row_num, onehot, precision=EXACT)
    part_den = jnp.dot(row_den, onehot, precision=EXACT)
    recv_num, recv_den = (
        lax.all_to_all(
            part_num.reshape(pen_size, per_owner), "pen", split_axis=0, concat_axis=0, tiled=True
        ),
        lax.all_to_all(
            part_den.reshape(pen_size, per_owner), "pen", split_axis=0, concat_axis=0, tiled=True
        ),
    )
    own_num = jnp.sum(recv_num, axis=0)
    own_den = jnp.sum(recv_den, axis=0)
    own_num, own_den = lax.psum((own_num, own_den), "gz")
    own_thrust = lax.dynamic_slice_in_dim(thrust, lax.axis_index("pen") * per_owner, per_owner)
    own_speed = own_num / own_den
    own_force = -0.5 * own_thrust * own_speed * jnp.abs(own_speed)
    disk_force = lax.all_gather(own_force, "pen", axis=0, tiled=True)
    row_force = jnp.dot(onehot, disk_force, precision=EXACT)
    cell_force = (row_force[:, None] * weights).reshape(-1)
    push_x = (
        jnp.zeros((levels * rows_here * length_x,), jnp.float32)
        .at[cells_flat.reshape(-1)]
        .add(cell_force)
    )
    push_x = push_x.reshape(levels, rows_here, length_x)
    tendency = jnp.stack(
        [
            smooth_v * spin_z - smooth_w * spin_y + push_x,
            smooth_w * spin_x - smooth_u * spin_z,
            smooth_u * spin_y - smooth_v * spin_x,
        ]
    )
    velocity_next = velocity + SECTION * tendency
    return (tendency, velocity_next)


LANES = 128
RADIX = 16
WHOLE_VMEM = 64 << 20


def rfft_parts(xs):
    n = len(xs)
    if n == 2:
        return [(xs[0] + xs[1], None), (xs[0] - xs[1], None)]
    even, odd = rfft_parts(xs[0::2]), rfft_parts(xs[1::2])
    out = [None] * (n // 2 + 1)
    out[0] = (even[0][0] + odd[0][0], None)
    out[n // 2] = (even[0][0] - odd[0][0], None)
    out[n // 4] = (even[n // 4][0], -odd[n // 4][0])
    for r in range(1, n // 4):
        (er, ei), (pr, pi) = even[r], odd[r]
        c, s = math.cos(2 * math.pi * r / n), math.sin(2 * math.pi * r / n)
        if 8 * r == n:
            tr, ti = (pr + pi) * c, (pi - pr) * c
        else:
            tr, ti = pr * c + pi * s, pi * c - pr * s
        out[r] = (er + tr, ei + ti)
        out[n // 2 - r] = (er - tr, ti - ei)
    return out


def irfft_parts(spec):
    n = 2 * (len(spec) - 1)
    if n == 2:
        return [spec[0][0] + spec[1][0], spec[0][0] - spec[1][0]]
    even, odd = [None] * (n // 4 + 1), [None] * (n // 4 + 1)
    even[0] = (spec[0][0] + spec[n // 2][0], None)
    odd[0] = (spec[0][0] - spec[n // 2][0], None)
    mid_re, mid_im = spec[n // 4]
    even[n // 4] = (2.0 * mid_re, None)
    odd[n // 4] = (-2.0 * mid_im, None)
    for r in range(1, n // 4):
        (ar, ai), (br, bi) = spec[r], spec[n // 2 - r]
        c, s = math.cos(2 * math.pi * r / n), math.sin(2 * math.pi * r / n)
        even[r] = (ar + br, ai - bi)
        dr, di = ar - br, ai + bi
        if 8 * r == n:
            odd[r] = ((dr - di) * c, (dr + di) * c)
        else:
            odd[r] = (dr * c - di * s, dr * s + di * c)
    out = [None] * n
    out[0::2] = irfft_parts(even)
    out[1::2] = irfft_parts(odd)
    return out


def halves(x):
    hi = x.astype(jnp.bfloat16)
    return hi, (x - hi.astype(jnp.float32)).astype(jnp.bfloat16)


def np_halves(x):
    x = np.asarray(x, np.float64)
    hi = x.astype(jnp.bfloat16)
    return hi, (x - hi.astype(np.float64)).astype(jnp.bfloat16)


class Plan:
    def __init__(self, length_x, length_y):
        modes = (length_x - 1) // 3 + 1
        self.length_x, self.length_y = length_x, length_y
        self.base = modes // RADIX
        self.width = 2 * self.base
        self.double, self.single = [], []
        for device in range(RADIX):
            pair, _ = pair_place(device)
            longer = [3 * (r + RADIX * self.base) < length_x for r in self.residues(pair)]
            (self.double if all(longer) else self.single).append(device)
        self.loose = [(device, self.width + i) for device in self.double for i in range(2)]
        self.guest = dict(zip(self.single, self.loose))
        self.hidden = self.loose[len(self.single):]

    def residues(self, pair):
        return pair, (RADIX - pair if pair else RADIX // 2)

    def lanes(self, pair):
        places, last = [], self.width
        for i, residue in enumerate(self.residues(pair)):
            places += [(i * self.base + m, residue + RADIX * m, i) for m in range(self.base)]
            if 3 * (residue + RADIX * self.base) < self.length_x:
                places.append((last, residue + RADIX * self.base, i))
                last += 1
        return places

    def x_weights(self):
        i = np.arange(LANES, dtype=np.int64)
        out = np.zeros((RADIX // 2, 2 * LANES, 2 * LANES))
        for pair in range(RADIX // 2):
            for lane, k, partner in self.lanes(pair):
                phase = 2 * np.pi * ((i * k) % self.length_x) / self.length_x
                c, s = np.cos(phase), np.sin(phase)
                for half, (on_re, on_im) in enumerate(((c, s), (-s, c))):
                    column = out[pair, :, half * LANES + lane]
                    if pair == 0:
                        column[partner * LANES:(partner + 1) * LANES] = on_re
                    else:
                        column[:LANES] = on_re
                        column[LANES:] = -on_im if partner else on_im
        return out

    def wave_lanes(self):
        out = np.zeros((RADIX // 2, LANES), np.float32)
        for pair in range(RADIX // 2):
            for lane, k, _ in self.lanes(pair):
                out[pair, lane] = 2 * np.pi * k / self.length_x
        return out

    def y_weights(self, rows):
        signed = np.arange(self.length_y)
        signed = np.where(signed <= self.length_y // 2, signed, signed - self.length_y)
        signed = signed[3 * np.abs(signed) < self.length_y]
        gap = np.arange(rows)[:, None] - np.arange(rows)[None, :]
        out = np.zeros((RADIX // 2, 4 * rows, 2 * rows))
        scale = 1.0 / (self.length_x * self.length_y)
        for pair in range(RADIX // 2):
            for op in range(2):
                blocks = []
                for residue in ((pair,) if pair else (0, RADIX // 2)):
                    chosen = signed[(signed - residue) % RADIX == 0]
                    phase = 2 * np.pi * ((gap[:, :, None] * chosen) % self.length_y) / self.length_y
                    kernel = np.exp(1j * phase)
                    if op:
                        kernel = kernel * (1j * 2 * np.pi * chosen / self.length_y)
                    blocks.append(kernel.sum(-1) * scale)
                base = 2 * rows * op
                if pair:
                    p = blocks[0]
                    full = np.block([[p.real, -p.imag], [p.imag, p.real]])
                else:
                    zero = np.zeros((rows, rows))
                    full = np.block([[blocks[0].real, zero], [zero, blocks[1].real]])
                out[pair, base:base + 2 * rows] = full
        return out


def triple(lhs_hi, lhs_lo, rhs_hi, rhs_lo, dims):
    lhs = jnp.concatenate([lhs_hi, lhs_hi, lhs_lo], axis=dims[0][0])
    rhs = jnp.concatenate([rhs_hi, rhs_lo, rhs_hi], axis=dims[1][0])
    return lax.dot_general(lhs, rhs, (dims, ((), ())), preferred_element_type=jnp.float32)


def pair_place(device):
    if device == 0 or device == RADIX // 2:
        return 0, (1 if device else 0)
    return (device, 0) if device < RADIX // 2 else (RADIX - device, 1)


def x_forward_kernel(plan, rows, vel_ref, whi_any, wlo_any, out_ref, whi_ref, wlo_ref, ahi, alo, spec, sems):
    comps = vel_ref.shape[0]
    step = 16
    loads = [
        pltpu.make_async_copy(whi_any, whi_ref, sems.at[0]),
        pltpu.make_async_copy(wlo_any, wlo_ref, sems.at[1]),
    ]
    for load in loads:
        load.start()

    def butterflies(g, carry):
        c = g // (rows // step)
        at = pl.multiple_of((g % (rows // step)) * step, step)
        block = [vel_ref[c, 0, pl.ds(at, step), j * LANES:(j + 1) * LANES] for j in range(RADIX)]
        parts = rfft_parts(block)
        row = pl.multiple_of(g * step, step)
        for pair in range(RADIX // 2):
            both = (parts[0][0], parts[RADIX // 2][0]) if pair == 0 else parts[pair]
            for half in range(2):
                hi, lo = halves(both[half])
                ahi[pair, pl.ds(row, step), half * LANES:(half + 1) * LANES] = hi
                alo[pair, pl.ds(row, step), half * LANES:(half + 1) * LANES] = lo
        return carry

    lax.fori_loop(0, comps * rows // step, butterflies, 0)
    for load in loads:
        load.wait()

    def multiply(pair, carry):
        spec[pair] = triple(ahi[pair], alo[pair], whi_ref[pair], wlo_ref[pair], ((1,), (0,)))
        return carry

    lax.fori_loop(0, RADIX // 2, multiply, 0, unroll=4)
    width = plan.width
    u_rest = 2 * width - LANES

    def pack(g, carry):
        at = pl.multiple_of(g * 8, 8)
        lane = lax.broadcasted_iota(jnp.int32, (8, LANES), 1)

        def tile(c, device):
            pair, half = pair_place(device)
            return spec[pair, pl.ds(c * rows + at, 8), half * LANES:(half + 1) * LANES]

        def turned(x, shift):
            return pltpu.roll(x, shift % LANES, 1)

        for p in range(RADIX):
            u, v, w = tile(0, p), tile(1, p), tile(2, p)
            if p == RADIX // 2:
                (one, lane_one), (two, lane_two) = plan.hidden
                u = jnp.where(lane == 0, turned(tile(1, one), -lane_one), u)
                w = jnp.where(lane == 0, turned(tile(1, two), -lane_two), w)
            moved_u = turned(u, width)
            first = jnp.where(lane < width, v, moved_u)
            second = jnp.where(lane < u_rest + 2, moved_u, turned(w, u_rest + 2))
            if p in plan.guest:
                other, other_lane = plan.guest[p]
                second = jnp.where(lane == u_rest + 1, turned(tile(1, other), u_rest + 1 - other_lane), second)
                second = jnp.where(lane == LANES - 1, turned(v, LANES - 1 - width), second)
            out_ref[p, pl.ds(at, 8), :] = first
            out_ref[p, pl.ds(rows + at, 8), :] = second
        return carry

    lax.fori_loop(0, rows // 8, pack, 0)


def y_kernel(plan, rows, in_ref, qhi_ref, qlo_ref, out_ref, ahi, alo, spec):
    step = 16

    def butterflies(g, carry):
        tile_index = g // (rows // step)
        at = pl.multiple_of((g % (rows // step)) * step, step)
        src = pl.multiple_of(g * step, step)
        parts = rfft_parts([in_ref[s, pl.ds(src, step), :] for s in range(RADIX)])
        for pair in range(RADIX // 2):
            both = (parts[0][0], parts[RADIX // 2][0]) if pair == 0 else parts[pair]
            for half in range(2):
                hi, lo = halves(both[half])
                ahi[tile_index, pair, pl.ds(half * rows + at, step), :] = hi
                alo[tile_index, pair, pl.ds(half * rows + at, step), :] = lo
        return carry

    lax.fori_loop(0, 2 * rows // step, butterflies, 0)

    def multiply(pair, carry):
        hi = jnp.concatenate([ahi[0, pair], ahi[1, pair]], axis=1)
        lo = jnp.concatenate([alo[0, pair], alo[1, pair]], axis=1)
        spec[pair] = triple(qhi_ref[pair], qlo_ref[pair], hi, lo, ((1,), (0,)))
        return carry

    lax.fori_loop(0, RADIX // 2, multiply, 0, unroll=4)
    width = plan.width

    def back(op, tile_index, at):
        cols = slice(tile_index * LANES, (tile_index + 1) * LANES)

        def part(pair, half):
            return spec[pair, pl.ds((2 * op + half) * rows + at, 8), cols]

        lines = [(part(0, 0), None)]
        lines += [(part(pair, 0), part(pair, 1)) for pair in range(1, RADIX // 2)]
        lines += [(part(0, 1), None)]
        return irfft_parts(lines)

    def finish(g, carry):
        at = pl.multiple_of(g * 8, 8)
        for block, (op, tile_index) in enumerate(((0, 0), (0, 1), (1, 1))):
            for s, value in enumerate(back(op, tile_index, at)):
                out_ref[s, pl.ds(block * rows + at, 8), :] = value
        return carry

    lax.fori_loop(0, rows // 8, finish, 0)

    def finish_half(g, carry):
        at = pl.multiple_of(g * 8, 8)
        lane = lax.broadcasted_iota(jnp.int32, (8, LANES), 1)
        upper, lower = back(1, 0, at), back(1, 0, at + rows // 2)
        for s in range(RADIX):
            both = jnp.where(lane >= width, upper[s], pltpu.roll(lower[s], LANES // 2, 1))
            out_ref[s, pl.ds(3 * rows + at, 8), :] = both
        return carry

    lax.fori_loop(0, rows // 16, finish_half, 0)


def x_back_kernel(
    plan, rows, slope_ref, in_ref, whi_any, wlo_any, wave_ref, vel_any, rim_any, push_any,
    tend_any, next_any,
    whi_ref, wlo_ref, vel_ref, rim_ref, push_ref, tend_ref, next_ref, lhi, llo, spec, phys, sems, out_sems,
):
    width, base = plan.width, plan.base
    step = 16
    u_rest = 2 * width - LANES
    sources = (whi_any, wlo_any, vel_any, rim_any, push_any)
    targets = (whi_ref, wlo_ref, vel_ref, rim_ref, push_ref)
    loads = [pltpu.make_async_copy(a, b, sems.at[i]) for i, (a, b) in enumerate(zip(sources, targets))]
    for load in loads:
        load.start()

    def unpack(upper, g, carry):
        at = pl.multiple_of(g * step, step)
        half_at = at if upper else pl.multiple_of(at - rows // 2, step)
        lane = lax.broadcasted_iota(jnp.int32, (step, LANES), 1)

        def turned(x, shift):
            return pltpu.roll(x, shift % LANES, 1)

        def first(p, op):
            if op == 0:
                return in_ref[p, pl.ds(at, step), :]
            both = in_ref[p, pl.ds(3 * rows + half_at, step), :]
            return both if upper else turned(both, LANES // 2)

        def second(p, op):
            return in_ref[p, pl.ds((1 + op) * rows + at, step), :]

        def u_tile(p, op):
            return turned(jnp.where(lane >= width, first(p, op), second(p, op)), -width)

        def w_tile(p, op):
            return turned(second(p, op), -(u_rest + 2))

        def v_tile(p):
            tile = first(p, 0)
            if p in plan.guest:
                own = turned(second(p, 0), width - LANES + 1)
                return jnp.where(lane >= width, own, tile)
            for host, (guest, guest_lane) in plan.guest.items():
                if guest == p:
                    moved = turned(second(host, 0), guest_lane - u_rest - 1)
                    tile = jnp.where(lane == guest_lane, moved, tile)
            for source, (guest, guest_lane) in zip((u_tile, w_tile), plan.hidden):
                if guest == p:
                    moved = turned(source(RADIX // 2, 0), guest_lane)
                    tile = jnp.where(lane == guest_lane, moved, tile)
            return tile

        for pair in range(RADIX // 2):
            a, b = plan.residues(pair)
            wave = wave_ref[pl.ds(pair, 1), :]
            va, vb, wa, wb = v_tile(a), v_tile(b), w_tile(a, 0), w_tile(b, 0)
            fields = (
                (u_tile(a, 0), u_tile(b, 0)),
                (va, vb),
                (wa, wb),
                (-wave * vb - u_tile(a, 1), wave * va - u_tile(b, 1)),
                (-wave * wb, wave * wa),
                (w_tile(a, 1), w_tile(b, 1)),
            )
            for f, both in enumerate(fields):
                row = pl.multiple_of(f * rows + at, step)
                for half, value in enumerate(both):
                    if pair == 0:
                        value = value * (2.0 if half else jnp.where(lane == 0, 1.0, 2.0))
                    hi, lo = halves(value)
                    lhi[pair, pl.ds(row, step), half * LANES:(half + 1) * LANES] = hi
                    llo[pair, pl.ds(row, step), half * LANES:(half + 1) * LANES] = lo
        return carry

    middle = rows // 2 // step
    lax.fori_loop(0, middle, functools.partial(unpack, True), 0)
    lax.fori_loop(middle, 2 * middle, functools.partial(unpack, False), 0)
    loads[0].wait()
    loads[1].wait()

    def multiply(pair, carry):
        spec[pair] = triple(lhi[pair], llo[pair], whi_ref[pair], wlo_ref[pair], ((1,), (1,)))
        return carry

    lax.fori_loop(0, RADIX // 2, multiply, 0, unroll=4)
    for load in loads[2:]:
        load.wait()
    z_scale = slope_ref[0]

    def stores(g):
        at = pl.multiple_of(g * 8, 8)
        part = (slice(None), slice(None), pl.ds(at, 8), slice(None))
        return [
            pltpu.make_async_copy(tend_ref.at[part], tend_any.at[part], out_sems.at[0, g]),
            pltpu.make_async_copy(next_ref.at[part], next_any.at[part], out_sems.at[1, g]),
        ]

    def finish(g, carry):
        at = pl.multiple_of(g * 8, 8)
        for f in range(6):
            def part(pair, half):
                return spec[pair, pl.ds(f * rows + at, 8), half * LANES:(half + 1) * LANES]

            lines = [(part(0, 0), None)]
            lines += [(part(pair, 0), part(pair, 1)) for pair in range(1, RADIX // 2)]
            lines += [(part(0, 1), None)]
            for j, value in enumerate(irfft_parts(lines)):
                phys[f, :, j * LANES:(j + 1) * LANES] = value
        for j in range(RADIX):
            cols = slice(j * LANES, (j + 1) * LANES)
            u, v, w, spin_z, w_x, w_y = [phys[f, :, cols] for f in range(6)]
            push = push_ref[j // 2, pl.ds(at, 8), (j % 2) * LANES:(j % 2 + 1) * LANES]
            spin_x = w_y - z_scale * rim_ref[1, 0, pl.ds(at, 8), cols]
            spin_y = z_scale * rim_ref[0, 0, pl.ds(at, 8), cols] - w_x
            rates = (v * spin_z - w * spin_y + push, w * spin_x - u * spin_z, u * spin_y - v * spin_x)
            for c, rate in enumerate(rates):
                tend_ref[c, 0, pl.ds(at, 8), cols] = rate
                next_ref[c, 0, pl.ds(at, 8), cols] = vel_ref[c, 0, pl.ds(at, 8), cols] + SECTION * rate
        for store in stores(g):
            store.start()
        return carry

    lax.fori_loop(0, rows // 8, finish, 0)

    def drain(g, carry):
        for store in stores(g):
            store.wait()
        return carry

    lax.fori_loop(0, rows // 8, drain, 0)


def cell_codes(cell, length_x):
    blocks = length_x // (2 * LANES)
    row, column = cell // length_x, cell % length_x
    return row, column // (2 * LANES), column % (2 * LANES), blocks


def sums_kernel(rows, vel_ref, cell_ref, owner_ref, weight_ref, out_ref, table_hi, table_lo, high, low, picked):
    length_x = vel_ref.shape[-1]
    blocks = length_x // (2 * LANES)
    for b in range(blocks):
        block = vel_ref[0, 0, :, b * 2 * LANES:(b + 1) * 2 * LANES]
        hi, lo = halves(block.T)
        table_hi[:, b * rows:(b + 1) * rows] = hi
        table_lo[:, b * rows:(b + 1) * rows] = lo
    row, block, lane_code, _ = cell_codes(cell_ref[0], length_x)
    high[...] = block * rows + row
    low[...] = lane_code
    cells = blocks * rows

    def gather(i, carry):
        h = jnp.concatenate([high[pl.ds(2 * i, 1), :], high[pl.ds(2 * i + 1, 1), :]], axis=1)
        l = jnp.concatenate([low[pl.ds(2 * i, 1), :], low[pl.ds(2 * i + 1, 1), :]], axis=1)
        hot = (lax.broadcasted_iota(jnp.int32, (cells, 2 * LANES), 0) == h).astype(jnp.float32).astype(jnp.bfloat16)
        found = jnp.dot(table_hi[...], hot, preferred_element_type=jnp.float32)
        found += jnp.dot(table_lo[...], hot, preferred_element_type=jnp.float32)
        mine = lax.broadcasted_iota(jnp.int32, (2 * LANES, 2 * LANES), 0) == l
        value = jnp.sum(jnp.where(mine, found, 0.0), axis=0, keepdims=True)
        picked[pl.ds(2 * i, 1), :] = value[:, :LANES]
        picked[pl.ds(2 * i + 1, 1), :] = value[:, LANES:]
        return carry

    lax.fori_loop(0, cell_ref.shape[1] // 2, gather, 0)
    weights = weight_ref[0]
    row_num = jnp.sum(weights * picked[...], axis=1, keepdims=True)
    row_den = jnp.sum(weights, axis=1, keepdims=True)
    mine = lax.broadcasted_iota(jnp.int32, weights.shape, 1) == owner_ref[0]
    num = jnp.sum(jnp.where(mine, row_num, 0.0), axis=0, keepdims=True)
    den = jnp.sum(jnp.where(mine, row_den, 0.0), axis=0, keepdims=True)
    out_ref[...] = jnp.concatenate([num, den, jnp.zeros((6, LANES), jnp.float32)], axis=0)


def push_kernel(rows, length_x, sum_ref, thrust_ref, cell_ref, owner_ref, weight_ref, out_ref, high, low, c_hi, c_lo, acc):
    blocks = length_x // (2 * LANES)
    cells = blocks * rows
    turbines = thrust_ref.shape[1]
    total = sum_ref[...]
    speed = total[0:1, :turbines] / total[1:2, :turbines]
    force = -0.5 * thrust_ref[...] * speed * jnp.abs(speed)
    mine = lax.broadcasted_iota(jnp.int32, (cell_ref.shape[1], turbines), 1) == owner_ref[0]
    row_force = jnp.sum(jnp.where(mine, force, 0.0), axis=1, keepdims=True)
    cell_force = row_force * weight_ref[0]
    big = cell_force.astype(jnp.bfloat16).astype(jnp.float32)
    c_hi[...] = big
    c_lo[...] = cell_force - big
    row, block, lane_code, _ = cell_codes(cell_ref[0], length_x)
    high[...] = block * rows + row
    low[...] = lane_code
    acc[...] = jnp.zeros_like(acc)

    def scatter(i, carry):
        def two(ref):
            return jnp.concatenate([ref[pl.ds(2 * i, 1), :], ref[pl.ds(2 * i + 1, 1), :]], axis=1)

        hot = (lax.broadcasted_iota(jnp.int32, (cells, 2 * LANES), 0) == two(high)).astype(jnp.float32).astype(jnp.bfloat16)
        mine = lax.broadcasted_iota(jnp.int32, (2 * LANES, 2 * LANES), 0) == two(low)
        upper = jnp.where(mine, two(c_hi), 0.0).astype(jnp.bfloat16)
        lower = jnp.where(mine, two(c_lo), 0.0).astype(jnp.bfloat16)
        dims = (((1,), (1,)), ((), ()))
        acc[...] += lax.dot_general(hot, upper, dims, preferred_element_type=jnp.float32) + lax.dot_general(
            hot, lower, dims, preferred_element_type=jnp.float32
        )
        return carry

    lax.fori_loop(0, cell_ref.shape[1] // 2, scatter, 0)
    for b in range(blocks):
        out_ref[b] = acc[b * rows:(b + 1) * rows, :]


def fits(velocity, sample_cell, thrust, pen_size):
    _, levels, rows, length_x = velocity.shape
    plan = Plan(length_x, rows * pen_size)
    return (
        pen_size == RADIX
        and levels == 1
        and 2 * rows == LANES
        and length_x == RADIX * LANES
        and sample_cell.shape[2] == LANES
        and sample_cell.shape[1] % 8 == 0
        and thrust.shape[0] <= LANES
        and 3 * plan.width + 4 == 2 * LANES
        and len(plan.hidden) == 2
    )


def mixed(value, masks):
    size = lax.axis_size("pen")
    moved = [lax.ppermute(value, "pen", [(i, i ^ mask) for i in range(size)]) for mask in masks]
    return value + sum(moved)


def packed_shards(velocity, inv_span, sample_cell, sample_turbine, sample_weight, thrust):
    comps, _, rows, length_x = velocity.shape
    pen_size = lax.axis_size("pen")
    plan = Plan(length_x, rows * pen_size)
    f32, bf16 = jnp.float32, jnp.bfloat16
    half = RADIX // 2
    wide = 2 * LANES
    w_hi, w_lo = [jnp.asarray(x) for x in np_halves(plan.x_weights())]
    q_hi, q_lo = [jnp.asarray(x) for x in np_halves(plan.y_weights(rows))]
    waves = jnp.asarray(plan.wave_lanes())
    shape = jax.ShapeDtypeStruct
    vmem = pltpu.VMEM
    whole = pl.BlockSpec(memory_space=pltpu.VMEM)
    anywhere = pl.BlockSpec(memory_space=pl.ANY)

    packed = pl.pallas_call(
        functools.partial(x_forward_kernel, plan, rows),
        out_shape=shape((RADIX, 2 * rows, LANES), f32),
        in_specs=[whole, anywhere, anywhere],
        out_specs=whole,
        scratch_shapes=[
            vmem(w_hi.shape, bf16),
            vmem(w_lo.shape, bf16),
            vmem((half, comps * rows, wide), bf16),
            vmem((half, comps * rows, wide), bf16),
            vmem((half, comps * rows, wide), f32),
            pltpu.SemaphoreType.DMA((2,)),
        ],
        name="x_forward",
    )(velocity, w_hi, w_lo)
    columns = lax.all_to_all(packed, "pen", split_axis=0, concat_axis=0, tiled=True)

    samples = sample_cell.shape[1]
    sample_scratch = [vmem((samples, LANES), jnp.int32)] * 2
    part = pl.pallas_call(
        functools.partial(sums_kernel, rows),
        out_shape=shape((8, LANES), f32),
        grid=(1,),
        in_specs=[
            pl.BlockSpec((1, 1, rows, length_x), lambda i: (0, 0, 0, 0)),
            pl.BlockSpec(sample_cell.shape, lambda i: (0, 0, 0)),
            pl.BlockSpec(sample_turbine.shape, lambda i: (0, 0, 0)),
            pl.BlockSpec(sample_weight.shape, lambda i: (0, 0, 0)),
        ],
        out_specs=pl.BlockSpec((8, LANES), lambda i: (0, 0)),
        scratch_shapes=[vmem((wide, length_x * rows // wide), bf16)] * 2
        + sample_scratch
        + [vmem((samples, LANES), f32)],
        compiler_params=pltpu.CompilerParams(vmem_limit_bytes=WHOLE_VMEM),
        name="disk_sums",
    )(velocity, sample_cell, sample_turbine, sample_weight)

    if lax.axis_size("gz") == 2:
        swap = [(0, 1), (1, 0)]
        rims = lax.ppermute(velocity[:2], "gz", swap)
        sign = 1.0 - 2.0 * lax.axis_index("gz").astype(f32)
        part = part + lax.ppermute(part, "gz", swap)
        scale = sign * inv_span
    else:
        around = padded(velocity[:2], (("gz", 1),), 1)
        rims = around[:, 2:] - around[:, :-2]
        part = lax.psum(part, "gz")
        scale = inv_span
    part = mixed(part, (1, 2, 3))
    part = mixed(part, (4, 8, 12))
    part, columns = lax.optimization_barrier((part, columns))
    answers = pl.pallas_call(
        functools.partial(y_kernel, plan, rows),
        out_shape=shape((RADIX, 3 * rows + rows // 2, LANES), f32),
        scratch_shapes=[
            vmem((2, half, 2 * rows, LANES), bf16),
            vmem((2, half, 2 * rows, LANES), bf16),
            vmem((half, 4 * rows, wide), f32),
        ],
        name="y_operators",
    )(columns, q_hi, q_lo)
    fields = lax.all_to_all(answers, "pen", split_axis=0, concat_axis=0, tiled=True)

    push = pl.pallas_call(
        functools.partial(push_kernel, rows, length_x),
        out_shape=shape((length_x // wide, rows, wide), f32),
        scratch_shapes=sample_scratch
        + [vmem((samples, LANES), f32)] * 2
        + [vmem((length_x * rows // wide, wide), f32)],
        compiler_params=pltpu.CompilerParams(vmem_limit_bytes=WHOLE_VMEM),
        name="disk_push",
    )(part, thrust[None], sample_cell, sample_turbine, sample_weight)

    out = shape(velocity.shape, f32)
    return pl.pallas_call(
        functools.partial(x_back_kernel, plan, rows),
        out_shape=(out, out),
        in_specs=[pl.BlockSpec(memory_space=pltpu.SMEM), whole, anywhere, anywhere, whole] + [anywhere] * 3,
        out_specs=(anywhere, anywhere),
        scratch_shapes=[
            vmem(w_hi.shape, bf16),
            vmem(w_lo.shape, bf16),
            vmem(velocity.shape, f32),
            vmem(rims.shape, f32),
            vmem(push.shape, f32),
            vmem(velocity.shape, f32),
            vmem(velocity.shape, f32),
            vmem((half, 6 * rows, wide), bf16),
            vmem((half, 6 * rows, wide), bf16),
            vmem((half, 6 * rows, wide), f32),
            vmem((6, 8, length_x), f32),
            pltpu.SemaphoreType.DMA((5,)),
            pltpu.SemaphoreType.DMA((2, rows // 8)),
        ],
        name="x_back",
    )(scale, fields, w_hi, w_lo, waves, velocity, rims, push)


def program(*arguments):
    velocity, sample_cell, thrust = arguments[0], arguments[2], arguments[5]
    if fits(velocity, sample_cell, thrust, lax.axis_size("pen")):
        return packed_shards(*arguments)
    return shards(*arguments)


def solution(mesh):
    return jax.shard_map(
        program,
        mesh=mesh,
        in_specs=(
            P(None, "gz", "pen", None),
            P("gz"),
            P("gz", "pen", None),
            P("gz", "pen", None),
            P("gz", "pen", None),
            P(),
        ),
        out_specs=(P(None, "gz", "pen", None), P(None, "gz", "pen", None)),
        check_vma=False,
    )
```

```python
import functools
import math

import jax
import jax.numpy as jnp
import numpy as np
from jax import lax
from jax.experimental import pallas as pl
from jax.experimental.pallas import tpu as pltpu
from jax.sharding import PartitionSpec as P

SAMP = 128


SECTION = 0.1
EXACT = lax.Precision.HIGHEST
RADIX_X = 64
RADIX_Y = 32


def padded(value, sides, width):
    for axis, dim in sides:
        size, length = (lax.axis_size(axis), value.shape[dim])
        up = [(i, (i + 1) % size) for i in range(size - 1)]
        down = [(j, i) for i, j in up]
        last = lax.slice_in_dim(value, length - width, length, axis=dim)
        first = lax.slice_in_dim(value, 0, width, axis=dim)
        before = lax.ppermute(last, axis, up)
        after = lax.ppermute(first, axis, down)
        value = jnp.concatenate([before, value, after], axis=dim)
    return value


def pair_table(first_index, second_index, length):
    angles = (first_index * second_index % length).astype(jnp.float32) * (2.0 * math.pi / length)
    return (jnp.cos(angles), jnp.sin(angles))


def shards(velocity, inv_span, sample_cell, sample_turbine, sample_weight, thrust):
    components, levels, rows_here, length_x = velocity.shape
    pen_size = lax.axis_size("pen")
    length_y = rows_here * pen_size
    top_y = (length_y - 1) // 3
    width_y = (2 * top_y + 128) // 128 * 128
    count = -(-((length_x - 1) // 3 + 1) // pen_size) * pen_size
    local = count // pen_size
    inner_x = length_x // RADIX_X
    blocks_x = -(-count // RADIX_X)
    cos_one_x, sin_one_x = pair_table(
        jnp.arange(RADIX_X, dtype=jnp.int32)[:, None],
        jnp.arange(RADIX_X, dtype=jnp.int32)[None, :],
        RADIX_X,
    )
    wave_slots = (
        jnp.arange(RADIX_X, dtype=jnp.int32)[None, :, None]
        + RADIX_X * jnp.arange(blocks_x, dtype=jnp.int32)[None, None, :]
    )
    cos_two_x, sin_two_x = pair_table(
        jnp.arange(inner_x, dtype=jnp.int32)[:, None, None], wave_slots, length_x
    )
    inner_y = length_y // RADIX_Y
    blocks_y = -(-width_y // RADIX_Y)
    cos_one_y, sin_one_y = pair_table(
        jnp.arange(RADIX_Y, dtype=jnp.int32)[:, None],
        jnp.arange(RADIX_Y, dtype=jnp.int32)[None, :] - top_y,
        RADIX_Y,
    )
    slot_grid = (
        jnp.arange(RADIX_Y, dtype=jnp.int32)[None, :, None]
        + RADIX_Y * jnp.arange(blocks_y, dtype=jnp.int32)[None, None, :]
    )
    usable = (slot_grid <= 2 * top_y).astype(jnp.float32)
    cos_two_y, sin_two_y = pair_table(
        jnp.arange(inner_y, dtype=jnp.int32)[:, None, None], slot_grid - top_y, length_y
    )
    cos_two_y = cos_two_y * usable
    sin_two_y = sin_two_y * usable
    wave_y = (jnp.arange(width_y, dtype=jnp.int32) - top_y).astype(jnp.float32) * (
        2.0 * math.pi / length_y
    )
    first_mode = lax.axis_index("pen") * local
    kept_x = (3 * (first_mode + jnp.arange(local, dtype=jnp.int32)) < length_x).astype(jnp.float32)
    rims = padded(velocity[:2], (("gz", 1),), 1)
    slopes_z = (rims[:, 2:] - rims[:, :-2]) * inv_span[None, :, None, None]
    folded = velocity.reshape(components, levels, rows_here, RADIX_X, inner_x)
    section_re = jnp.einsum("czyji,jk->czyik", folded, cos_one_x, precision=EXACT)
    section_im = -jnp.einsum("czyji,jk->czyik", folded, sin_one_x, precision=EXACT)
    four_re = jnp.einsum("czyik,ikm->czymk", section_re, cos_two_x, precision=EXACT) + jnp.einsum(
        "czyik,ikm->czymk", section_im, sin_two_x, precision=EXACT
    )
    four_im = jnp.einsum("czyik,ikm->czymk", section_im, cos_two_x, precision=EXACT) - jnp.einsum(
        "czyik,ikm->czymk", section_re, sin_two_x, precision=EXACT
    )
    spectra = jnp.stack([four_re, four_im], axis=1).reshape(
        components, 2, levels, rows_here, blocks_x * RADIX_X
    )
    spectra = jnp.transpose(spectra[..., :count], (0, 1, 2, 4, 3))
    spectra = spectra.reshape(components, 2, levels, 1, count * rows_here)
    pencil_block = lax.all_to_all(spectra, "pen", split_axis=4, concat_axis=3, tiled=True)
    depth_here = pencil_block.shape[2]
    pencils = pencil_block.reshape(components, 2, depth_here, pen_size, local, rows_here)
    lines = jnp.transpose(pencils, (0, 1, 2, 4, 3, 5)).reshape(
        components, 2, depth_here, local, RADIX_Y, inner_y
    )
    line_re = lines[:, 0]
    line_im = lines[:, 1]
    part_re = jnp.einsum("czkji,js->czkis", line_re, cos_one_y, precision=EXACT) + jnp.einsum(
        "czkji,js->czkis", line_im, sin_one_y, precision=EXACT
    )
    part_im = jnp.einsum("czkji,js->czkis", line_im, cos_one_y, precision=EXACT) - jnp.einsum(
        "czkji,js->czkis", line_re, sin_one_y, precision=EXACT
    )
    mode_re = jnp.einsum("czkis,ist->czkts", part_re, cos_two_y, precision=EXACT) + jnp.einsum(
        "czkis,ist->czkts", part_im, sin_two_y, precision=EXACT
    )
    mode_im = jnp.einsum("czkis,ist->czkts", part_im, cos_two_y, precision=EXACT) - jnp.einsum(
        "czkis,ist->czkts", part_re, sin_two_y, precision=EXACT
    )
    mode_values = jnp.stack([mode_re, mode_im], axis=1).reshape(
        components, 2, depth_here, local, blocks_y * RADIX_Y
    )
    mode_values = mode_values * kept_x[None, None, None, :, None]
    paired = jnp.stack([mode_values[0], mode_values[2]])
    slopes = jnp.stack([-wave_y * paired[:, 1], wave_y * paired[:, 0]], axis=1)
    stacked = jnp.concatenate([mode_values, slopes], axis=0) * (1.0 / length_y)
    stacked = stacked.reshape(5, 2, depth_here, local, blocks_y, RADIX_Y)
    back_re = stacked[:, 0]
    back_im = stacked[:, 1]
    half_re = jnp.einsum("fzkts,ist->fzkis", back_re, cos_two_y, precision=EXACT) - jnp.einsum(
        "fzkts,ist->fzkis", back_im, sin_two_y, precision=EXACT
    )
    half_im = jnp.einsum("fzkts,ist->fzkis", back_re, sin_two_y, precision=EXACT) + jnp.einsum(
        "fzkts,ist->fzkis", back_im, cos_two_y, precision=EXACT
    )
    line_back_re = jnp.einsum("fzkis,js->fzkji", half_re, cos_one_y, precision=EXACT) - jnp.einsum(
        "fzkis,js->fzkji", half_im, sin_one_y, precision=EXACT
    )
    line_back_im = jnp.einsum("fzkis,js->fzkji", half_re, sin_one_y, precision=EXACT) + jnp.einsum(
        "fzkis,js->fzkji", half_im, cos_one_y, precision=EXACT
    )
    pencils_back = jnp.stack([line_back_re, line_back_im], axis=1).reshape(
        5, 2, depth_here, local, pen_size, rows_here
    )
    pencils_back = jnp.transpose(pencils_back, (0, 1, 2, 4, 3, 5)).reshape(
        5, 2, depth_here, pen_size, local * rows_here
    )
    fields = lax.all_to_all(pencils_back, "pen", split_axis=3, concat_axis=3, tiled=True)
    fields = fields.reshape(5, 2, levels, count, rows_here)
    wave_x = (jnp.arange(count, dtype=jnp.float32) * (2.0 * math.pi / length_x))[None, :, None]
    filter_u = fields[0]
    filter_v = fields[1]
    filter_w = fields[2]
    slope_uy = fields[3]
    slope_wy = fields[4]
    spin_hat = jnp.stack([-wave_x * filter_v[1] - slope_uy[0], wave_x * filter_v[0] - slope_uy[1]])
    slope_hat = jnp.stack([-wave_x * filter_w[1], wave_x * filter_w[0]])
    sixfold = jnp.stack([filter_u, filter_v, filter_w, spin_hat, slope_hat, slope_wy])
    factor = jnp.where(jnp.arange(count) == 0, 1.0, 2.0) / length_x
    sixfold = sixfold * factor[None, None, None, :, None]
    sixfold = jnp.pad(sixfold, ((0, 0), (0, 0), (0, 0), (0, blocks_x * RADIX_X - count), (0, 0)))
    sixfold = sixfold.reshape(6, 2, levels, blocks_x, RADIX_X, rows_here)
    six_re = sixfold[:, 0]
    six_im = sixfold[:, 1]
    mix_re = jnp.einsum("fzmky,ikm->fzyik", six_re, cos_two_x, precision=EXACT) - jnp.einsum(
        "fzmky,ikm->fzyik", six_im, sin_two_x, precision=EXACT
    )
    mix_im = jnp.einsum("fzmky,ikm->fzyik", six_re, sin_two_x, precision=EXACT) + jnp.einsum(
        "fzmky,ikm->fzyik", six_im, cos_two_x, precision=EXACT
    )
    physical = jnp.einsum("fzyik,jk->fzyji", mix_re, cos_one_x, precision=EXACT) - jnp.einsum(
        "fzyik,jk->fzyji", mix_im, sin_one_x, precision=EXACT
    )
    physical = physical.reshape(6, levels, rows_here, length_x)
    smooth_u = physical[0]
    smooth_v = physical[1]
    smooth_w = physical[2]
    spin_z = physical[3]
    w_slope_x = physical[4]
    w_slope_y = physical[5]
    spin_x = w_slope_y - slopes_z[1]
    spin_y = slopes_z[0] - w_slope_x
    row_count = sample_cell.shape[1]
    cells_flat = sample_cell.reshape(row_count, SAMP)
    weights = sample_weight.reshape(row_count, SAMP)
    picked = velocity[0].reshape(-1)[cells_flat]
    weighted = weights * picked
    owners = sample_turbine.reshape(row_count)
    turbines = thrust.shape[0]
    per_owner = turbines // pen_size
    owner_match = owners[:, None] == jnp.arange(turbines, dtype=jnp.int32)[None, :]
    onehot = owner_match.astype(jnp.float32)
    row_num = jnp.sum(weighted, axis=1)
    row_den = jnp.sum(weights, axis=1)
    part_num = jnp.dot(row_num, onehot, precision=EXACT)
    part_den = jnp.dot(row_den, onehot, precision=EXACT)
    recv_num, recv_den = (
        lax.all_to_all(
            part_num.reshape(pen_size, per_owner), "pen", split_axis=0, concat_axis=0, tiled=True
        ),
        lax.all_to_all(
            part_den.reshape(pen_size, per_owner), "pen", split_axis=0, concat_axis=0, tiled=True
        ),
    )
    own_num = jnp.sum(recv_num, axis=0)
    own_den = jnp.sum(recv_den, axis=0)
    own_num, own_den = lax.psum((own_num, own_den), "gz")
    own_thrust = lax.dynamic_slice_in_dim(thrust, lax.axis_index("pen") * per_owner, per_owner)
    own_speed = own_num / own_den
    own_force = -0.5 * own_thrust * own_speed * jnp.abs(own_speed)
    disk_force = lax.all_gather(own_force, "pen", axis=0, tiled=True)
    row_force = jnp.dot(onehot, disk_force, precision=EXACT)
    cell_force = (row_force[:, None] * weights).reshape(-1)
    push_x = (
        jnp.zeros((levels * rows_here * length_x,), jnp.float32)
        .at[cells_flat.reshape(-1)]
        .add(cell_force)
    )
    push_x = push_x.reshape(levels, rows_here, length_x)
    tendency = jnp.stack(
        [
            smooth_v * spin_z - smooth_w * spin_y + push_x,
            smooth_w * spin_x - smooth_u * spin_z,
            smooth_u * spin_y - smooth_v * spin_x,
        ]
    )
    velocity_next = velocity + SECTION * tendency
    return (tendency, velocity_next)


LANES = 128
RADIX = 16
UNROLL = 4
WHOLE_VMEM = 64 << 20


def rfft_parts(xs):
    n = len(xs)
    if n == 2:
        return [(xs[0] + xs[1], None), (xs[0] - xs[1], None)]
    even, odd = rfft_parts(xs[0::2]), rfft_parts(xs[1::2])
    out = [None] * (n // 2 + 1)
    out[0] = (even[0][0] + odd[0][0], None)
    out[n // 2] = (even[0][0] - odd[0][0], None)
    out[n // 4] = (even[n // 4][0], -odd[n // 4][0])
    for r in range(1, n // 4):
        (er, ei), (pr, pi) = even[r], odd[r]
        c, s = math.cos(2 * math.pi * r / n), math.sin(2 * math.pi * r / n)
        if 8 * r == n:
            tr, ti = (pr + pi) * c, (pi - pr) * c
        else:
            tr, ti = pr * c + pi * s, pi * c - pr * s
        out[r] = (er + tr, ei + ti)
        out[n // 2 - r] = (er - tr, ti - ei)
    return out


def irfft_parts(spec):
    n = 2 * (len(spec) - 1)
    if n == 2:
        return [spec[0][0] + spec[1][0], spec[0][0] - spec[1][0]]
    even, odd = [None] * (n // 4 + 1), [None] * (n // 4 + 1)
    even[0] = (spec[0][0] + spec[n // 2][0], None)
    odd[0] = (spec[0][0] - spec[n // 2][0], None)
    mid_re, mid_im = spec[n // 4]
    even[n // 4] = (2.0 * mid_re, None)
    odd[n // 4] = (-2.0 * mid_im, None)
    for r in range(1, n // 4):
        (ar, ai), (br, bi) = spec[r], spec[n // 2 - r]
        c, s = math.cos(2 * math.pi * r / n), math.sin(2 * math.pi * r / n)
        even[r] = (ar + br, ai - bi)
        dr, di = ar - br, ai + bi
        if 8 * r == n:
            odd[r] = ((dr - di) * c, (dr + di) * c)
        else:
            odd[r] = (dr * c - di * s, dr * s + di * c)
    out = [None] * n
    out[0::2] = irfft_parts(even)
    out[1::2] = irfft_parts(odd)
    return out


def halves(x):
    hi = x.astype(jnp.bfloat16)
    return hi, (x - hi.astype(jnp.float32)).astype(jnp.bfloat16)


def np_halves(x):
    x = np.asarray(x, np.float64)
    hi = x.astype(jnp.bfloat16)
    return hi, (x - hi.astype(np.float64)).astype(jnp.bfloat16)


class Plan:
    def __init__(self, length_x, length_y):
        modes = (length_x - 1) // 3 + 1
        self.length_x, self.length_y = length_x, length_y
        self.base = modes // RADIX
        self.width = 2 * self.base
        self.double, self.single = [], []
        for device in range(RADIX):
            pair, _ = pair_place(device)
            longer = [3 * (r + RADIX * self.base) < length_x for r in self.residues(pair)]
            (self.double if all(longer) else self.single).append(device)
        self.loose = [(device, self.width + i) for device in self.double for i in range(2)]
        self.guest = dict(zip(self.single, self.loose))
        self.hidden = self.loose[len(self.single):]

        pairs = sorted({pair_place(d)[0] for d in self.double} - {0}) + [0]
        pairs += sorted({pair_place(d)[0] for d in self.single})
        self.order = [(self.residues(pair), pair) for pair in pairs]

    def residues(self, pair):
        return pair, (RADIX - pair if pair else RADIX // 2)

    def lanes(self, pair):
        places, last = [], self.width
        for i, residue in enumerate(self.residues(pair)):
            places += [(i * self.base + m, residue + RADIX * m, i) for m in range(self.base)]
            if 3 * (residue + RADIX * self.base) < self.length_x:
                places.append((last, residue + RADIX * self.base, i))
                last += 1
        return places

    def x_weights(self):
        i = np.arange(LANES, dtype=np.int64)
        out = np.zeros((RADIX // 2, 2 * LANES, 2 * LANES))
        for pair in range(RADIX // 2):
            for lane, k, partner in self.lanes(pair):
                phase = 2 * np.pi * ((i * k) % self.length_x) / self.length_x
                c, s = np.cos(phase), np.sin(phase)
                for half, (on_re, on_im) in enumerate(((c, s), (-s, c))):
                    column = out[pair, :, half * LANES + lane]
                    if pair == 0:
                        column[partner * LANES:(partner + 1) * LANES] = on_re
                    else:
                        column[:LANES] = on_re
                        column[LANES:] = -on_im if partner else on_im
        return out

    def wave_lanes(self):
        out = np.zeros((RADIX // 2, LANES), np.float32)
        for pair in range(RADIX // 2):
            for lane, k, _ in self.lanes(pair):
                out[pair, lane] = 2 * np.pi * k / self.length_x
        return out

    def y_weights(self, rows):
        signed = np.arange(self.length_y)
        signed = np.where(signed <= self.length_y // 2, signed, signed - self.length_y)
        signed = signed[3 * np.abs(signed) < self.length_y]
        gap = np.arange(rows)[:, None] - np.arange(rows)[None, :]
        out = np.zeros((RADIX // 2, 4 * rows, 2 * rows))
        scale = 1.0 / (self.length_x * self.length_y)
        for pair in range(RADIX // 2):
            for op in range(2):
                blocks = []
                for residue in ((pair,) if pair else (0, RADIX // 2)):
                    chosen = signed[(signed - residue) % RADIX == 0]
                    phase = 2 * np.pi * ((gap[:, :, None] * chosen) % self.length_y) / self.length_y
                    kernel = np.exp(1j * phase)
                    if op:
                        kernel = kernel * (1j * 2 * np.pi * chosen / self.length_y)
                    blocks.append(kernel.sum(-1) * scale)
                base = 2 * rows * op
                if pair:
                    p = blocks[0]
                    full = np.block([[p.real, -p.imag], [p.imag, p.real]])
                else:
                    zero = np.zeros((rows, rows))
                    full = np.block([[blocks[0].real, zero], [zero, blocks[1].real]])
                out[pair, base:base + 2 * rows] = full
        return out


def triple(lhs_hi, lhs_lo, rhs_hi, rhs_lo, dims):
    lhs = jnp.concatenate([lhs_hi, lhs_hi, lhs_lo], axis=dims[0][0])
    rhs = jnp.concatenate([rhs_hi, rhs_lo, rhs_hi], axis=dims[1][0])
    return lax.dot_general(lhs, rhs, (dims, ((), ())), preferred_element_type=jnp.float32)


def pair_place(device):
    if device == 0 or device == RADIX // 2:
        return 0, (1 if device else 0)
    return (device, 0) if device < RADIX // 2 else (RADIX - device, 1)


def x_forward_kernel(
    plan, rows, vel_any, whi_any, wlo_any, out_any, vel_ref, whi_ref, wlo_ref, out_ref, ahi, alo, spec, sems, out_sems
):
    comps = vel_ref.shape[0]
    step = 16
    loads = [pltpu.make_async_copy(vel_any.at[c], vel_ref.at[c], sems.at[c]) for c in range(comps)]
    loads.append(pltpu.make_async_copy(whi_any, whi_ref, sems.at[comps]))
    loads.append(pltpu.make_async_copy(wlo_any, wlo_ref, sems.at[comps + 1]))
    for load in loads:
        load.start()

    def butterflies(c, g, carry):
        at = pl.multiple_of(g * step, step)
        block = [vel_ref[c, 0, pl.ds(at, step), j * LANES:(j + 1) * LANES] for j in range(RADIX)]
        parts = rfft_parts(block)
        row = pl.multiple_of(c * rows + g * step, step)
        for pair in range(RADIX // 2):
            both = (parts[0][0], parts[RADIX // 2][0]) if pair == 0 else parts[pair]
            for half in range(2):
                hi, lo = halves(both[half])
                ahi[pair, pl.ds(row, step), half * LANES:(half + 1) * LANES] = hi
                alo[pair, pl.ds(row, step), half * LANES:(half + 1) * LANES] = lo
        return carry

    for c in range(comps):
        loads[c].wait()
        lax.fori_loop(0, rows // step, functools.partial(butterflies, c), 0)
    for load in loads[comps:]:
        load.wait()
    width = plan.width
    u_rest = 2 * width - LANES
    lane = lax.broadcasted_iota(jnp.int32, (8, LANES), 1)

    def turned(x, shift):
        return pltpu.roll(x, shift % LANES, 1)

    def pack(p):
        for at in range(0, rows, 8):
            def tile(c, device):
                pair, half = pair_place(device)
                return spec[pair, c * rows + at:c * rows + at + 8, half * LANES:(half + 1) * LANES]

            u, v, w = tile(0, p), tile(1, p), tile(2, p)
            if p == RADIX // 2:
                (one, lane_one), (two, lane_two) = plan.hidden
                u = jnp.where(lane == 0, turned(tile(1, one), -lane_one), u)
                w = jnp.where(lane == 0, turned(tile(1, two), -lane_two), w)
            moved_u = turned(u, width)
            first = jnp.where(lane < width, v, moved_u)
            second = jnp.where(lane < u_rest + 2, moved_u, turned(w, u_rest + 2))
            if p in plan.guest:
                other, other_lane = plan.guest[p]
                second = jnp.where(lane == u_rest + 1, turned(tile(1, other), u_rest + 1 - other_lane), second)
                second = jnp.where(lane == LANES - 1, turned(v, LANES - 1 - width), second)
            out_ref[p, at:at + 8, :] = first
            out_ref[p, rows + at:rows + at + 8, :] = second

    stores = []
    for devices, pair in plan.order:
        spec[pair] = triple(ahi[pair], alo[pair], whi_ref[pair], wlo_ref[pair], ((1,), (0,)))
        for p in devices:
            pack(p)
            stores.append(pltpu.make_async_copy(out_ref.at[p], out_any.at[p], out_sems.at[p]))
            stores[-1].start()
    for store in stores:
        store.wait()


def y_kernel(plan, rows, in_any, qhi_any, qlo_any, out_any, in_ref, qhi_ref, qlo_ref, out_ref, ahi, alo, spec, sems, out_sems):
    step = 16
    tiles = [pl.ds(0, rows), pl.ds(rows, rows)]
    loads = [pltpu.make_async_copy(in_any.at[:, tiles[i], :], in_ref.at[:, tiles[i], :], sems.at[i]) for i in range(2)]
    loads.append(pltpu.make_async_copy(qhi_any, qhi_ref, sems.at[2]))
    loads.append(pltpu.make_async_copy(qlo_any, qlo_ref, sems.at[3]))
    for load in loads:
        load.start()

    def butterflies(tile_index, g, carry):
        at = pl.multiple_of(g * step, step)
        src = pl.multiple_of(tile_index * rows + g * step, step)
        parts = rfft_parts([in_ref[s, pl.ds(src, step), :] for s in range(RADIX)])
        for pair in range(RADIX // 2):
            both = (parts[0][0], parts[RADIX // 2][0]) if pair == 0 else parts[pair]
            for half in range(2):
                hi, lo = halves(both[half])
                ahi[tile_index, pair, pl.ds(half * rows + at, step), :] = hi
                alo[tile_index, pair, pl.ds(half * rows + at, step), :] = lo
        return carry

    for tile_index in range(2):
        loads[tile_index].wait()
        lax.fori_loop(0, rows // step, functools.partial(butterflies, tile_index), 0)
    loads[2].wait()
    loads[3].wait()

    def multiply(pair, carry):
        hi = jnp.concatenate([ahi[0, pair], ahi[1, pair]], axis=1)
        lo = jnp.concatenate([alo[0, pair], alo[1, pair]], axis=1)
        spec[pair] = triple(qhi_ref[pair], qlo_ref[pair], hi, lo, ((1,), (0,)))
        return carry

    lax.fori_loop(0, RADIX // 2, multiply, 0, unroll=4)
    width = plan.width

    def back(op, tile_index, at):
        cols = slice(tile_index * LANES, (tile_index + 1) * LANES)

        def part(pair, half):
            return spec[pair, pl.ds((2 * op + half) * rows + at, 8), cols]

        lines = [(part(0, 0), None)]
        lines += [(part(pair, 0), part(pair, 1)) for pair in range(1, RADIX // 2)]
        lines += [(part(0, 1), None)]
        return irfft_parts(lines)

    blocks = []
    for block, (op, tile_index) in enumerate(((0, 0), (0, 1), (1, 1), (1, 0))):
        size = rows if block < 3 else rows // 2
        part = pl.ds(block * rows, size)
        blocks.append((op, tile_index, pltpu.make_async_copy(out_ref.at[:, part, :], out_any.at[:, part, :], out_sems.at[block])))

    def finish(block, op, tile_index, g, carry):
        at = pl.multiple_of(g * 8, 8)
        for s, value in enumerate(back(op, tile_index, at)):
            out_ref[s, pl.ds(block * rows + at, 8), :] = value
        return carry

    def finish_half(g, carry):
        at = pl.multiple_of(g * 8, 8)
        lane = lax.broadcasted_iota(jnp.int32, (8, LANES), 1)
        upper, lower = back(1, 0, at), back(1, 0, at + rows // 2)
        for s in range(RADIX):
            both = jnp.where(lane >= width, upper[s], pltpu.roll(lower[s], LANES // 2, 1))
            out_ref[s, pl.ds(3 * rows + at, 8), :] = both
        return carry

    for block, (op, tile_index, store) in enumerate(blocks):
        if block < 3:
            lax.fori_loop(0, rows // 8, functools.partial(finish, block, op, tile_index), 0, unroll=2)
        else:
            lax.fori_loop(0, rows // 16, finish_half, 0)
        store.start()
    for _, _, store in blocks:
        store.wait()


def x_back_kernel(
    plan, rows, slope_ref, in_any, whi_any, wlo_any, wave_ref, vel_any, rim_any, push_any,
    tend_any, next_any,
    in_ref, whi_ref, wlo_ref, vel_ref, rim_ref, push_ref, tend_ref, next_ref, lhi, llo, spec, phys, in_sems, sems, out_sems,
):
    width, base = plan.width, plan.base
    step = 16
    u_rest = 2 * width - LANES
    chunks = [pltpu.make_async_copy(in_any.at[p], in_ref.at[p], in_sems.at[p]) for p in range(RADIX)]
    order = plan.order[::-1]
    for devices, _ in order:
        for p in devices:
            chunks[p].start()
    sources = (whi_any, wlo_any, vel_any, rim_any, push_any)
    targets = (whi_ref, wlo_ref, vel_ref, rim_ref, push_ref)
    loads = [pltpu.make_async_copy(a, b, sems.at[i]) for i, (a, b) in enumerate(zip(sources, targets))]
    for load in loads[:2]:
        load.start()
    lane = lax.broadcasted_iota(jnp.int32, (step, LANES), 1)

    def turned(x, shift):
        return pltpu.roll(x, shift % LANES, 1)

    def unpack(pair, at):
        def first(p, op):
            if op == 0:
                return in_ref[p, at:at + step, :]
            upper = at < rows // 2
            start = 3 * rows + at % (rows // 2)
            both = in_ref[p, start:start + step, :]
            return both if upper else turned(both, LANES // 2)

        def second(p, op):
            return in_ref[p, (1 + op) * rows + at:(1 + op) * rows + at + step, :]

        def u_tile(p, op):
            return turned(jnp.where(lane >= width, first(p, op), second(p, op)), -width)

        def w_tile(p, op):
            return turned(second(p, op), -(u_rest + 2))

        def v_tile(p):
            tile = first(p, 0)
            if p in plan.guest:
                own = turned(second(p, 0), width - LANES + 1)
                return jnp.where(lane >= width, own, tile)
            for host, (guest, guest_lane) in plan.guest.items():
                if guest == p:
                    moved = turned(second(host, 0), guest_lane - u_rest - 1)
                    tile = jnp.where(lane == guest_lane, moved, tile)
            for source, (guest, guest_lane) in zip((u_tile, w_tile), plan.hidden):
                if guest == p:
                    moved = turned(source(RADIX // 2, 0), guest_lane)
                    tile = jnp.where(lane == guest_lane, moved, tile)
            return tile

        a, b = plan.residues(pair)
        wave = wave_ref[pair:pair + 1, :]
        va, vb, wa, wb = v_tile(a), v_tile(b), w_tile(a, 0), w_tile(b, 0)
        fields = (
            (u_tile(a, 0), u_tile(b, 0)),
            (va, vb),
            (wa, wb),
            (-wave * vb - u_tile(a, 1), wave * va - u_tile(b, 1)),
            (-wave * wb, wave * wa),
            (w_tile(a, 1), w_tile(b, 1)),
        )
        for f, both in enumerate(fields):
            row = f * rows + at
            for half, value in enumerate(both):
                if pair == 0:
                    value = value * (2.0 if half else jnp.where(lane == 0, 1.0, 2.0))
                hi, lo = halves(value)
                lhi[pair, row:row + step, half * LANES:(half + 1) * LANES] = hi
                llo[pair, row:row + step, half * LANES:(half + 1) * LANES] = lo

    for chunk in chunks:
        chunk.wait()
    for position, (_, pair) in enumerate(order):
        for at in range(0, rows, step):
            unpack(pair, at)
        if position == 0:
            for load in loads[:2]:
                load.wait()
            for load in loads[2:]:
                load.start()
        spec[pair] = triple(lhi[pair], llo[pair], whi_ref[pair], wlo_ref[pair], ((1,), (0,)))
    for load in loads[2:]:
        load.wait()
    z_scale = slope_ref[0]

    def stores(g):
        at = pl.multiple_of(g * 8, 8)
        part = (slice(None), slice(None), pl.ds(at, 8), slice(None))
        return [
            pltpu.make_async_copy(tend_ref.at[part], tend_any.at[part], out_sems.at[0, g]),
            pltpu.make_async_copy(next_ref.at[part], next_any.at[part], out_sems.at[1, g]),
        ]

    def finish(g, carry):
        at = pl.multiple_of(g * 8, 8)
        for f in range(6):
            def part(pair, half):
                return spec[pair, pl.ds(f * rows + at, 8), half * LANES:(half + 1) * LANES]

            lines = [(part(0, 0), None)]
            lines += [(part(pair, 0), part(pair, 1)) for pair in range(1, RADIX // 2)]
            lines += [(part(0, 1), None)]
            for j, value in enumerate(irfft_parts(lines)):
                phys[f, :, j * LANES:(j + 1) * LANES] = value
        for j in range(RADIX):
            cols = slice(j * LANES, (j + 1) * LANES)
            u, v, w, spin_z, w_x, w_y = [phys[f, :, cols] for f in range(6)]
            push = push_ref[j // 2, pl.ds(at, 8), (j % 2) * LANES:(j % 2 + 1) * LANES]
            spin_x = w_y - z_scale * rim_ref[1, 0, pl.ds(at, 8), cols]
            spin_y = z_scale * rim_ref[0, 0, pl.ds(at, 8), cols] - w_x
            rates = (v * spin_z - w * spin_y + push, w * spin_x - u * spin_z, u * spin_y - v * spin_x)
            for c, rate in enumerate(rates):
                tend_ref[c, 0, pl.ds(at, 8), cols] = rate
                next_ref[c, 0, pl.ds(at, 8), cols] = vel_ref[c, 0, pl.ds(at, 8), cols] + SECTION * rate
        for store in stores(g):
            store.start()
        return carry

    lax.fori_loop(0, rows // 8, finish, 0)

    def drain(g, carry):
        for store in stores(g):
            store.wait()
        return carry

    lax.fori_loop(0, rows // 8, drain, 0)


def cell_codes(cell, length_x):
    wide = 2 * LANES
    row = lax.shift_right_logical(cell, length_x.bit_length() - 1)
    block = lax.shift_right_logical(cell & (length_x - 1), wide.bit_length() - 1)
    return row, block, cell & (wide - 1)


def owners_column(owner_ref, count):
    row = owner_ref[0].astype(jnp.float32)
    shape = (count, count)
    same = lax.broadcasted_iota(jnp.int32, shape, 0) == lax.broadcasted_iota(jnp.int32, shape, 1)
    return jnp.sum(jnp.where(same, row, 0.0), axis=1, keepdims=True).astype(jnp.int32)


def unit_square():
    shape = (2 * LANES, 2 * LANES)
    same = lax.broadcasted_iota(jnp.int32, shape, 0) == lax.broadcasted_iota(jnp.int32, shape, 1)
    return same.astype(jnp.float32).astype(jnp.bfloat16)


def flipped(unit, value):
    out = lax.dot_general(unit, value, (((1,), (1,)), ((), ())), preferred_element_type=jnp.float32)
    return out.astype(jnp.bfloat16)


def two_rows(ref, i):
    return jnp.concatenate([ref[pl.ds(2 * i, 1), :], ref[pl.ds(2 * i + 1, 1), :]], axis=1)


def one_hot(codes, size):
    places = lax.broadcasted_iota(jnp.int32, (size, 2 * LANES), 0)
    return (places == codes).astype(jnp.float32).astype(jnp.bfloat16)


def sums_kernel(rows, vel_ref, cell_ref, owner_ref, weight_ref, out_ref, table, lines, high, low, picked):
    length_x = vel_ref.shape[-1]
    blocks = length_x // (2 * LANES)
    cells = blocks * rows
    for b in range(blocks):
        hi, lo = halves(vel_ref[0, 0, :, b * 2 * LANES:(b + 1) * 2 * LANES])
        lines[b * rows:(b + 1) * rows, :] = hi
        lines[cells + b * rows:cells + (b + 1) * rows, :] = lo
    table[:2 * LANES, :] = flipped(unit_square(), lines[:cells, :])
    table[2 * LANES:, :] = flipped(unit_square(), lines[cells:, :])
    row, block, lane_code = cell_codes(cell_ref[0], length_x)
    high[...] = block * rows + row
    low[...] = lane_code

    def gather(i, carry):
        hot = one_hot(two_rows(high, i), cells)
        both = jnp.dot(table[...], hot, preferred_element_type=jnp.float32)
        found = both[:2 * LANES] + both[2 * LANES:]
        mine = lax.broadcasted_iota(jnp.int32, (2 * LANES, 2 * LANES), 0) == two_rows(low, i)
        value = jnp.sum(jnp.where(mine, found, 0.0), axis=0, keepdims=True)
        picked[pl.ds(2 * i, 1), :] = value[:, :LANES]
        picked[pl.ds(2 * i + 1, 1), :] = value[:, LANES:]
        return carry

    lax.fori_loop(0, cell_ref.shape[1] // 2, gather, 0, unroll=UNROLL)
    weights = weight_ref[0]
    row_num = jnp.sum(weights * picked[...], axis=1, keepdims=True)
    row_den = jnp.sum(weights, axis=1, keepdims=True)
    mine = lax.broadcasted_iota(jnp.int32, weights.shape, 1) == owners_column(owner_ref, weights.shape[0])
    num = jnp.sum(jnp.where(mine, row_num, 0.0), axis=0, keepdims=True)
    den = jnp.sum(jnp.where(mine, row_den, 0.0), axis=0, keepdims=True)
    out_ref[...] = jnp.concatenate([num, den, jnp.zeros((6, LANES), jnp.float32)], axis=0)


def push_kernel(
    rows, length_x, sum_ref, thrust_ref, cell_ref, owner_ref, weight_ref, whi_ref, wlo_ref,
    out_ref, thi_ref, tlo_ref, high, low, c_hi, c_lo, acc,
):
    blocks = length_x // (2 * LANES)
    cells = blocks * rows
    turbines = thrust_ref.shape[1]
    total = sum_ref[...]
    speed = total[0:1, :turbines] / total[1:2, :turbines]
    force = -0.5 * thrust_ref[...] * speed * jnp.abs(speed)
    mine = lax.broadcasted_iota(jnp.int32, (cell_ref.shape[1], turbines), 1) == owners_column(owner_ref, cell_ref.shape[1])
    row_force = jnp.sum(jnp.where(mine, force, 0.0), axis=1, keepdims=True)
    cell_force = row_force * weight_ref[0]
    big = cell_force.astype(jnp.bfloat16).astype(jnp.float32)
    c_hi[...] = big
    c_lo[...] = cell_force - big
    row, block, lane_code = cell_codes(cell_ref[0], length_x)
    high[...] = block * rows + row
    low[...] = lane_code
    acc[...] = jnp.zeros_like(acc)

    def scatter(i, carry):
        hot = one_hot(two_rows(high, i), cells)
        mine = lax.broadcasted_iota(jnp.int32, (2 * LANES, 2 * LANES), 0) == two_rows(low, i)
        upper = jnp.where(mine, two_rows(c_hi, i), 0.0).astype(jnp.bfloat16)
        lower = jnp.where(mine, two_rows(c_lo, i), 0.0).astype(jnp.bfloat16)
        dims = (((1,), (1,)), ((), ()))
        acc[...] += lax.dot_general(hot, upper, dims, preferred_element_type=jnp.float32) + lax.dot_general(
            hot, lower, dims, preferred_element_type=jnp.float32
        )
        return carry

    lax.fori_loop(0, cell_ref.shape[1] // 2, scatter, 0)
    for b in range(blocks):
        out_ref[b] = acc[b * rows:(b + 1) * rows, :]

    def turn(pair, carry):
        unit = unit_square()
        thi_ref[pair] = flipped(unit, whi_ref[pair])
        tlo_ref[pair] = flipped(unit, wlo_ref[pair])
        return carry

    lax.fori_loop(0, whi_ref.shape[0], turn, 0)


def fits(velocity, sample_cell, thrust, pen_size):
    _, levels, rows, length_x = velocity.shape
    plan = Plan(length_x, rows * pen_size)
    return (
        pen_size == RADIX
        and levels == 1
        and 2 * rows == LANES
        and length_x == RADIX * LANES
        and sample_cell.shape[2] == LANES
        and sample_cell.shape[1] % 8 == 0
        and thrust.shape[0] <= LANES
        and 3 * plan.width + 4 == 2 * LANES
        and len(plan.hidden) == 2
    )


def mixed(value, masks):
    size = lax.axis_size("pen")
    moved = [lax.ppermute(value, "pen", [(i, i ^ mask) for i in range(size)]) for mask in masks]
    return value + sum(moved)


def packed_shards(velocity, inv_span, sample_cell, sample_turbine, sample_weight, thrust):
    comps, _, rows, length_x = velocity.shape
    pen_size = lax.axis_size("pen")
    plan = Plan(length_x, rows * pen_size)
    f32, bf16 = jnp.float32, jnp.bfloat16
    half = RADIX // 2
    wide = 2 * LANES
    w_hi, w_lo = [jnp.asarray(x) for x in np_halves(plan.x_weights())]
    q_hi, q_lo = [jnp.asarray(x) for x in np_halves(plan.y_weights(rows))]
    waves = jnp.asarray(plan.wave_lanes())
    shape = jax.ShapeDtypeStruct
    vmem = pltpu.VMEM
    whole = pl.BlockSpec(memory_space=pltpu.VMEM)
    anywhere = pl.BlockSpec(memory_space=pl.ANY)

    packed = pl.pallas_call(
        functools.partial(x_forward_kernel, plan, rows),
        out_shape=shape((RADIX, 2 * rows, LANES), f32),
        in_specs=[anywhere] * 3,
        out_specs=anywhere,
        scratch_shapes=[
            vmem(velocity.shape, f32),
            vmem(w_hi.shape, bf16),
            vmem(w_lo.shape, bf16),
            vmem((RADIX, 2 * rows, LANES), f32),
            vmem((half, comps * rows, wide), bf16),
            vmem((half, comps * rows, wide), bf16),
            vmem((half, comps * rows, wide), f32),
            pltpu.SemaphoreType.DMA((comps + 2,)),
            pltpu.SemaphoreType.DMA((RADIX,)),
        ],
        name="x_forward",
    )(velocity, w_hi, w_lo)
    columns = lax.all_to_all(packed, "pen", split_axis=0, concat_axis=0, tiled=True)

    samples = sample_cell.shape[1]
    owners = sample_turbine.reshape(1, 1, samples)
    sample_scratch = [vmem((samples, LANES), jnp.int32)] * 2
    part = pl.pallas_call(
        functools.partial(sums_kernel, rows),
        out_shape=shape((8, LANES), f32),
        grid=(1,),
        in_specs=[
            pl.BlockSpec((1, 1, rows, length_x), lambda i: (0, 0, 0, 0)),
            pl.BlockSpec(sample_cell.shape, lambda i: (0, 0, 0)),
            pl.BlockSpec(owners.shape, lambda i: (0, 0, 0)),
            pl.BlockSpec(sample_weight.shape, lambda i: (0, 0, 0)),
        ],
        out_specs=pl.BlockSpec((8, LANES), lambda i: (0, 0)),
        scratch_shapes=[vmem((2 * wide, length_x * rows // wide), bf16), vmem((2 * length_x * rows // wide, wide), bf16)]
        + sample_scratch
        + [vmem((samples, LANES), f32)],
        compiler_params=pltpu.CompilerParams(vmem_limit_bytes=WHOLE_VMEM),
        name="disk_sums",
    )(velocity, sample_cell, owners, sample_weight)

    if lax.axis_size("gz") == 2:
        swap = [(0, 1), (1, 0)]
        rims = lax.ppermute(velocity[:2], "gz", swap)
        sign = 1.0 - 2.0 * lax.axis_index("gz").astype(f32)
        part = part + lax.ppermute(part, "gz", swap)
        scale = sign * inv_span
    else:
        around = padded(velocity[:2], (("gz", 1),), 1)
        rims = around[:, 2:] - around[:, :-2]
        part = lax.psum(part, "gz")
        scale = inv_span
    part = mixed(part, (1, 2, 3))
    part = mixed(part, (4, 8, 12))
    part, columns = lax.optimization_barrier((part, columns))
    answers = pl.pallas_call(
        functools.partial(y_kernel, plan, rows),
        out_shape=shape((RADIX, 3 * rows + rows // 2, LANES), f32),
        in_specs=[anywhere] * 3,
        out_specs=anywhere,
        scratch_shapes=[
            vmem(columns.shape, f32),
            vmem(q_hi.shape, bf16),
            vmem(q_lo.shape, bf16),
            vmem((RADIX, 3 * rows + rows // 2, LANES), f32),
            vmem((2, half, 2 * rows, LANES), bf16),
            vmem((2, half, 2 * rows, LANES), bf16),
            vmem((half, 4 * rows, wide), f32),
            pltpu.SemaphoreType.DMA((4,)),
            pltpu.SemaphoreType.DMA((4,)),
        ],
        name="y_operators",
    )(columns, q_hi, q_lo)
    fields = lax.all_to_all(answers, "pen", split_axis=0, concat_axis=0, tiled=True)

    push, t_hi, t_lo = pl.pallas_call(
        functools.partial(push_kernel, rows, length_x),
        out_shape=(shape((length_x // wide, rows, wide), f32), shape(w_hi.shape, bf16), shape(w_lo.shape, bf16)),
        scratch_shapes=sample_scratch
        + [vmem((samples, LANES), f32)] * 2
        + [vmem((length_x * rows // wide, wide), f32)],
        compiler_params=pltpu.CompilerParams(vmem_limit_bytes=WHOLE_VMEM),
        name="disk_push",
    )(part, thrust[None], sample_cell, owners, sample_weight, w_hi, w_lo)

    out = shape(velocity.shape, f32)
    return pl.pallas_call(
        functools.partial(x_back_kernel, plan, rows),
        out_shape=(out, out),
        in_specs=[pl.BlockSpec(memory_space=pltpu.SMEM), anywhere, anywhere, anywhere, whole] + [anywhere] * 3,
        out_specs=(anywhere, anywhere),
        scratch_shapes=[
            vmem(fields.shape, f32),
            vmem(w_hi.shape, bf16),
            vmem(w_lo.shape, bf16),
            vmem(velocity.shape, f32),
            vmem(rims.shape, f32),
            vmem(push.shape, f32),
            vmem(velocity.shape, f32),
            vmem(velocity.shape, f32),
            vmem((half, 6 * rows, wide), bf16),
            vmem((half, 6 * rows, wide), bf16),
            vmem((half, 6 * rows, wide), f32),
            vmem((6, 8, length_x), f32),
            pltpu.SemaphoreType.DMA((RADIX,)),
            pltpu.SemaphoreType.DMA((5,)),
            pltpu.SemaphoreType.DMA((2, rows // 8)),
        ],
        name="x_back",
    )(scale, fields, t_hi, t_lo, waves, velocity, rims, push)


def program(*arguments):
    velocity, sample_cell, thrust = arguments[0], arguments[2], arguments[5]
    if fits(velocity, sample_cell, thrust, lax.axis_size("pen")):
        return packed_shards(*arguments)
    return shards(*arguments)


def solution(mesh):
    return jax.shard_map(
        program,
        mesh=mesh,
        in_specs=(
            P(None, "gz", "pen", None),
            P("gz"),
            P("gz", "pen", None),
            P("gz", "pen", None),
            P("gz", "pen", None),
            P(),
        ),
        out_specs=(P(None, "gz", "pen", None), P(None, "gz", "pen", None)),
        check_vma=False,
    )
```
